512 devices in a mesh: gx: 16 (over x, y), gy: 32 (over z, core).
Axes of the slice: x: 4, y: 4, z: 16, core: 2. Of those that a mesh axis runs over, the one named last changes fastest.
Arguments:
- right_side: float32 [128, 256, 256], P('gx', 'gy'), may hold values from -6 to 6
- coefficient: float32 [128, 256, 256], P('gx', 'gy'), may hold values from 0.5 to 4
Outputs:
- solution_field: float32 [128, 256, 256], P('gx', 'gy')
The draws below stay inside these ranges and needn't reach their ends.
All inputs are finite; a program needn't handle non-finite values.
Results may differ from the reference program's by a relative error of at most 0.000078.
Values sent between devices are 32-bit elements; how exact they have to be, the bound alone decides.
A program may use at most 64 MiB of HBM per device.

```python
import math
import jax
import jax.numpy as jnp
from jax import lax

NZ = 256
LEVELS = 3
SMOOTH = 2
COARSE_STEPS = 6
NX = 128
NY = 256


def draw_right_side(key, part):
    rough_part = jax.random.normal(key, (NX, NY, NZ), jnp.float32)
    return jnp.clip(rough_part, -6.0, 6.0)


def level_of(rng, shape, pieces, smallest, top_value):
    def one(position, blocks):
        steps = jax.random.uniform(jax.random.fold_in(jax.random.fold_in(rng, 6), position), (blocks,), jnp.float32, smallest / len(pieces), top_value / len(pieces))
        return jnp.repeat(jnp.exp(steps), shape[position] // blocks).reshape((-1,) + (1,) * (len(shape) - position - 1))

    loudness = one(*pieces[0])
    for cut in pieces[1:]:
        loudness = loudness * one(*cut)
    return loudness


def setup_inputs(seed: int = 0) -> dict:
    seeds = jax.random.split(jax.random.key(seed), 3)
    return {
        "right_side": draw_right_side(jax.random.fold_in(seeds[2], 71), 0),
        "coefficient": jnp.clip(jnp.exp(math.log(4.0) - 2.0794415 * jax.random.uniform(seeds[1], (NX, NY, NZ), jnp.float32) ** level_of(seeds[1], (NX, NY, NZ), ((0, 16), (1, 32)), -0.2, 0.2)), 0.5, 4.0),
    }


SMOOTH_LOW = 0.5
SMOOTH_HIGH = 2.0
COARSE_LOW = 0.05
COARSE_HIGH = 2.0


def chebyshev(low_end, high_end, sweeps):
    middle = 0.5 * (high_end + low_end)
    half_span = 0.5 * (high_end - low_end)
    sig_ratio = middle / half_span
    rho_now = 1.0 / sig_ratio
    coeff_pairs = []
    for sweep_num in range(1, sweeps):
        rho_next = 1.0 / (2.0 * sig_ratio - rho_now)
        coeff_pairs.append((rho_next * rho_now, 2.0 * rho_next / half_span))
        rho_now = rho_next
    return 1.0 / middle, coeff_pairs


def neighbours(padded):
    return [padded[2:, 1:-1, 1:-1], padded[:-2, 1:-1, 1:-1], padded[1:-1, 2:, 1:-1],
            padded[1:-1, :-2, 1:-1], padded[1:-1, 1:-1, 2:], padded[1:-1, 1:-1, :-2]]


def face_weights(padded):
    centre = padded[1:-1, 1:-1, 1:-1]
    weights = [0.5 * (centre + beside_cell) for beside_cell in neighbours(padded)]
    diagonal = weights[0] + weights[1] + weights[2] + weights[3] + weights[4] + weights[5]
    return weights, diagonal


def apply_operator(padded, weights, diagonal):
    beside_list = neighbours(padded)
    summed = weights[0] * beside_list[0]
    for face_num in range(1, 6):
        summed = summed + weights[face_num] * beside_list[face_num]
    return diagonal * padded[1:-1, 1:-1, 1:-1] - summed


def restrict_sum(field):
    field = field[0::2] + field[1::2]
    field = field[:, 0::2] + field[:, 1::2]
    return field[:, :, 0::2] + field[:, :, 1::2]


def prolong_axis(padded, axis_num):
    length = padded.shape[axis_num] - 2
    centre = lax.slice_in_dim(padded, 1, length + 1, axis=axis_num)
    before = lax.slice_in_dim(padded, 0, length, axis=axis_num)
    following = lax.slice_in_dim(padded, 2, length + 2, axis=axis_num)
    even_part = 0.75 * centre + 0.25 * before
    odd_part = 0.75 * centre + 0.25 * following
    joined = jnp.stack([even_part, odd_part], axis=axis_num + 1)
    new_shape = list(centre.shape)
    new_shape[axis_num] = 2 * length
    return joined.reshape(new_shape)


def prolong_whole(coarse):
    padded = jnp.pad(coarse, 1)
    for axis_num in range(3):
        padded = prolong_axis(padded, axis_num)
    return padded


def residual_whole(iterate, source, weights, diagonal):
    return source - apply_operator(jnp.pad(iterate, 1), weights, diagonal)


def smooth_whole(iterate, source, weights, diagonal, low_end, high_end, sweeps):
    inverse = 1.0 / diagonal
    inv_mid, coeff_pairs = chebyshev(low_end, high_end, sweeps)
    residue = source if iterate is None else residual_whole(iterate, source, weights, diagonal)
    step_dir = residue * inverse * inv_mid
    iterate = step_dir if iterate is None else iterate + step_dir
    for keep_part, push_part in coeff_pairs:
        residue = residual_whole(iterate, source, weights, diagonal)
        step_dir = keep_part * step_dir + push_part * (residue * inverse)
        iterate = iterate + step_dir
    return iterate


def reference(right_side, coefficient):
    source = right_side
    coeffs = coefficient
    stored = []
    for level_num in range(LEVELS - 1):
        weights, diagonal = face_weights(jnp.pad(coeffs, 1))
        iterate = smooth_whole(None, source, weights, diagonal, SMOOTH_LOW, SMOOTH_HIGH, SMOOTH)
        residue = residual_whole(iterate, source, weights, diagonal)
        stored.append((iterate, source, weights, diagonal))
        source = 0.5 * restrict_sum(residue)
        coeffs = 0.125 * restrict_sum(coeffs)
    weights, diagonal = face_weights(jnp.pad(coeffs, 1))
    coarse = smooth_whole(None, source, weights, diagonal, COARSE_LOW, COARSE_HIGH, COARSE_STEPS)
    residue = residual_whole(coarse, source, weights, diagonal)
    ones_image = apply_operator(jnp.pad(jnp.ones_like(source), 1), weights, diagonal)
    coarse = coarse + jnp.sum(residue) / jnp.sum(ones_image)
    for iterate, source, weights, diagonal in reversed(stored):
        iterate = iterate + prolong_whole(coarse)
        coarse = smooth_whole(iterate, source, weights, diagonal, SMOOTH_LOW, SMOOTH_HIGH, SMOOTH)
    return coarse
```

```python
import jax
import jax.numpy as jnp
from jax import lax
from jax.experimental import pallas as pl
from jax.experimental.pallas import tpu as pltpu
from jax.sharding import PartitionSpec as P

SMOOTH_LOW = 0.5
SMOOTH_HIGH = 2.0
COARSE_LOW = 0.05
COARSE_HIGH = 2.0
COARSE_STEPS = 6

F32 = jnp.float32
NXD, NYD = 16, 32
NX, NY, NZ = 128, 256, 256
R5 = 5
R4 = 4
MESH = pl.DeviceIdType.MESH
NEAR = [(a, b) for a in (-1, 0, 1) for b in (-1, 0, 1) if (a, b) != (0, 0)]


def chebyshev(low_end, high_end, sweeps):
    middle = 0.5 * (high_end + low_end)
    half_span = 0.5 * (high_end - low_end)
    sig_ratio = middle / half_span
    rho_now = 1.0 / sig_ratio
    pairs = []
    for _ in range(1, sweeps):
        rho_next = 1.0 / (2.0 * sig_ratio - rho_now)
        pairs.append((rho_next * rho_now, 2.0 * rho_next / half_span))
        rho_now = rho_next
    return 1.0 / middle, pairs


def iota(shape, dim):
    return lax.broadcasted_iota(jnp.int32, shape, dim)


def dot(a, b):
    return jnp.dot(a, b, precision=lax.Precision.HIGHEST, preferred_element_type=F32)


def up1(v):
    return pltpu.roll(v, v.shape[0] - 1, 0)


def dn1(v):
    return pltpu.roll(v, 1, 0)


def lup(v):
    return pltpu.roll(v, v.shape[1] - 1, 1)


def ldn(v):
    return pltpu.roll(v, 1, 1)


def interp(out_cell, in_cell):
    home = out_cell >> 1
    near = jnp.where((out_cell & 1) == 0, home - 1, home + 1)
    return jnp.where(in_cell == home, 0.75, 0.0).astype(F32) + jnp.where(in_cell == near, 0.25, 0.0).astype(F32)


def pair_sum(fine, coarse):
    r, c = iota((fine, coarse), 0), iota((fine, coarse), 1)
    return jnp.where((r >> 1) == c, 1.0, 0.0).astype(F32)


class Level:
    def __init__(self, refs, planes, rows, lanes, zfull):
        self.c, self.wx, self.wy, self.wz, self.dg, self.iv = refs
        self.planes, self.rows, self.lanes, self.zfull = planes, rows, lanes, zfull

    def build(self, mask_of, lo, hi):
        lane = iota((self.rows, self.lanes), 1)
        c = self.c[lo - 1]
        for i in range(lo - 1, hi):
            nxt = self.c[i + 1]
            wxp = 0.5 * (c + nxt)
            self.wx[i] = wxp
            if i >= lo:
                wyp = 0.5 * (c + up1(c))
                wym = dn1(wyp)
                if self.zfull:
                    wzp = 0.5 * (c + jnp.where(lane == self.lanes - 1, 0.0, lup(c)))
                    wzm = 0.5 * (c + jnp.where(lane == 0, 0.0, ldn(c)))
                    wz = jnp.where(lane == self.lanes - 1, 0.0, wzp)
                else:
                    wzp = 0.5 * (c + lup(c))
                    wzm = ldn(wzp)
                    wz = wzp
                diag = wxp + self.wx[i - 1] + wyp + wym + wzp + wzm
                m = mask_of(i)
                self.wy[i] = wyp
                self.wz[i] = wz
                self.dg[i] = diag
                self.iv[i] = m / jnp.where(m > 0.5, diag, 1.0)
            c = nxt

    def apply(self, v, i):
        x = v[i]
        s = self.wx[i] * v[i + 1] + self.wx[i - 1] * v[i - 1]
        wy = self.wy[i]
        s = s + wy * up1(x) + dn1(wy * x)
        wz = self.wz[i]
        s = s + wz * lup(x) + ldn(wz * x)
        return self.dg[i] * x - s


def body_kernel(f_ref, c_ref, o_ref,
                sy, rxf, rxc, ry, rcf, rcc, f0, v0a, v0b, l0,
                sc1, rc1, sf1, rf1, su1, ru1, f1, u1, v1a, v1b, l1,
                sc2, gc2, ac2, sf2, gf2, af2, f2, v2a, v2b, d2, l2,
                r0b, r1b, lp1, lp0, rz0, rz1, pz1, pz0,
                sg1, rg1, sg2, rg2, ssem, rsem, gsem):
    mx, my = lax.axis_index("gx"), lax.axis_index("gy")

    def dev(a, b):
        return (lax.rem(mx + (a + NXD), NXD), lax.rem(my + (b + NYD), NYD))

    partners = [(a, b) for a, b in NEAR if a and b]
    partners += [(0, b) for b in range(1, NYD)] + [(a, 0) for a in range(1, NXD)]
    barrier = pltpu.get_barrier_semaphore()
    for a, b in partners:
        pl.semaphore_signal(barrier, inc=1, device_id=dev(a, b), device_id_type=MESH)

    sends = []

    def send(src, dst, a, b):
        k = len(sends)
        copy = pltpu.make_async_remote_copy(src_ref=src, dst_ref=dst, send_sem=ssem.at[k], recv_sem=rsem.at[k],
                                            device_id=dev(a, b), device_id_type=MESH)
        copy.start()
        sends.append(copy)
        return copy

    for p in range(8):
        fp, cp = f_ref[p], c_ref[p]
        for s in (0, 1):
            sy[s, 0, p] = fp[4 * s : 4 * s + 4]
            sy[s, 1, p] = cp[4 * s : 4 * s + 4]
    rz0[...] = pair_sum(256, 128)
    rz1[...] = pair_sum(128, 128)
    o, q = iota((16, 64), 0), iota((16, 64), 1)
    lc1 = jnp.where(((q >> 4) == (o >> 2)) & (((q & 7) >> 1) == (o & 3)), 0.125, 0.0).astype(F32)
    c1own = dot(dot(lc1, c_ref[...].reshape(64, 256)), rz0[...])
    sc1[...] = c1own.reshape(4, 4, 128)
    o, q = iota((4, 16), 0), iota((4, 16), 1)
    lc2 = jnp.where(((q >> 3) == (o >> 1)) & (((q & 3) >> 1) == (o & 1)), 0.125, 0.0).astype(F32)
    sc2[...] = dot(dot(lc2, c1own), rz1[...])
    zed = jnp.zeros((16, 256), F32)
    for p in (0, 1, 2, 3, 12, 13, 14, 15):
        f0[p] = zed
        l0[0][p] = zed
    pl.semaphore_wait(barrier, len(partners))

    wait_a = []
    for s, a in ((1, 1), (0, -1)):
        wait_a.append(send(c_ref.at[4:8] if s else c_ref.at[0:4], rxc.at[1 - s], a, 0))
        wait_a.append(send(f_ref.at[5:8] if s else f_ref.at[0:3], rxf.at[1 - s], a, 0))
    for sx, a in ((1, 1), (0, -1)):
        for s, b in ((1, 1), (0, -1)):
            wait_a.append(send(sy.at[s, 1, 5:8] if sx else sy.at[s, 1, 0:3], rcc.at[1 - sx, 1 - s], a, b))
            wait_a.append(send(sy.at[s, 0, 6:8] if sx else sy.at[s, 0, 0:2], rcf.at[1 - sx, 1 - s], a, b))
    for s, b in ((1, 1), (0, -1)):
        wait_a.append(send(sy.at[s], ry.at[1 - s], 0, b))
    offs5 = [k for k in range(-R5, R5 + 1) if k]
    offs4 = [k for k in range(-R4, R4 + 1) if k]
    wait_c2 = [send(sc2, gc2.at[R5 - k], 0, k) for k in offs5]
    wait_c1 = [send(sc1, rc1.at[n], a, b) for n, (a, b) in enumerate(NEAR)]

    o, q = iota((16, 128), 0), iota((16, 128), 1)
    yr = (q & 15) - 4
    lr0 = jnp.where(((q >> 5) == (o >> 2)) & ((yr >> 1) == (o & 3)) & (yr >= 0) & (yr < 8), 0.5, 0.0).astype(F32)
    o, q = iota((4, 64), 0), iota((4, 64), 1)
    yr = (q & 15) - 4
    lr1 = jnp.where(((q >> 5) == (o >> 1)) & ((yr >> 1) == (o & 1)) & (yr >= 0) & (yr < 4), 0.5, 0.0).astype(F32)

    def prolong_matrix(planes_out, x_out0, x_in0, rows_in, planes_in, y_out0, y_in0, bx, by, nx, ny):
        shape = (planes_out * 16, planes_in * rows_in)
        r, c = iota(shape, 0), iota(shape, 1)
        xo, yo = (r >> 4) + x_out0, (r & 15) + y_out0
        if rows_in == 16:
            ci, cr = c >> 4, c & 15
        else:
            ci = (c * 2731) >> 16
            cr = c - ci * rows_in
        w = interp(xo, ci + x_in0) * interp(yo, cr + y_in0)
        gx_, gy_ = xo + mx * bx, yo + my * by
        ok = (gx_ >= 0) & (gx_ < nx) & (gy_ >= 0) & (gy_ < ny)
        return jnp.where(ok, w, 0.0)

    lp1[...] = prolong_matrix(12, -4, -3, 24, 8, -4, -10, 4, 4, 64, 128)
    lp0[...] = prolong_matrix(12, -2, -2, 16, 8, -4, -4, 8, 8, 128, 256)
    r, c = iota((128, 128), 0), iota((128, 128), 1)
    pz1[...] = jnp.where(r < 64, interp(c, r), 0.0)
    r, c = iota((128, 256), 0), iota((128, 256), 1)
    pz0[...] = interp(c, r)

    def masker(rows, lanes, halo, b, nx, ny, valid_lanes, valid_rows):
        row = iota((rows, lanes), 0)
        y = row - halo + my * b
        ok = (y >= 0) & (y < ny) & (row < valid_rows)
        if valid_lanes < lanes:
            ok = ok & (iota((rows, lanes), 1) < valid_lanes)
        base = jnp.where(ok, 1.0, 0.0).astype(F32)

        def mask_of(i):
            x = mx * b + (i - halo)
            return base * jnp.where((x >= 0) & (x < nx), 1.0, 0.0).astype(F32)

        return mask_of

    mask0 = masker(16, 256, 4, 8, NX, NY, 256, 16)
    mask1 = masker(16, 128, 4, 4, NX // 2, NY // 2, 128, 12)
    mask2 = masker(24, 128, 10, 2, NX // 4, NY // 4, 64, 22)

    def spread2(mine, got, rows, cells, offs):
        rows[0, 20:24] = jnp.zeros((4, 128), F32)
        rows[1, 20:24] = jnp.zeros((4, 128), F32)
        for k in [0] + offs:
            g = mine[...] if k == 0 else got[k + R5]
            for x in (0, 1):
                rows[x, 2 * (k + R5) : 2 * (k + R5) + 2] = g[2 * x : 2 * x + 2]
        cells[10] = rows[0]
        cells[11] = rows[1]

    for w in wait_c2:
        w.wait_recv()
    spread2(sc2, gc2, ac2, l2[0], offs5)
    wait_c2 = [send(ac2, l2[0].at[2 * (R5 - k) : 2 * (R5 - k) + 2], k, 0) for k in offs5]

    for w in wait_a:
        w.wait_recv()
    c0 = l0[0]
    for p in range(8):
        i = p + 4
        f0[i, 0:4] = ry[0, 0, p]
        f0[i, 4:12] = f_ref[p]
        f0[i, 12:16] = ry[1, 0, p]
        c0[i, 0:4] = ry[0, 1, p]
        c0[i, 4:12] = c_ref[p]
        c0[i, 12:16] = ry[1, 1, p]
    for p in range(4):
        c0[p, 4:12] = rxc[0, p]
        c0[12 + p, 4:12] = rxc[1, p]
    for p in range(3):
        f0[1 + p, 4:12] = rxf[0, p]
        f0[12 + p, 4:12] = rxf[1, p]
        for s in (0, 1):
            c0[1 + p, 12 * s : 12 * s + 4] = rcc[0, s, p]
            c0[12 + p, 12 * s : 12 * s + 4] = rcc[1, s, p]
    for p in range(2):
        for s in (0, 1):
            f0[2 + p, 12 * s : 12 * s + 4] = rcf[0, s, p]
            f0[12 + p, 12 * s : 12 * s + 4] = rcf[1, s, p]
    for i in range(16):
        c0[i] = c0[i] * mask0(i)
    lev0 = Level(l0, 16, 16, 256, True)
    lev0.build(mask0, 1, 15)

    inv_mid, ((keep, push),) = chebyshev(SMOOTH_LOW, SMOOTH_HIGH, 2)

    def first(lev, f, v, lo, hi):
        for i in range(lo, hi):
            v[i] = f[i] * lev.iv[i] * inv_mid

    def second(lev, f, va, vb, lo, hi):
        for i in range(lo, hi):
            d = va[i]
            r = f[i] - lev.apply(va, i)
            vb[i] = d + (keep * d + push * (r * lev.iv[i]))

    def residual(lev, f, v, out, lo, hi):
        for i in range(lo, hi):
            out[i - lo] = f[i] - lev.apply(v, i)

    v0a[0] = zed
    v0a[15] = zed
    first(lev0, f0, v0a, 1, 15)
    second(lev0, f0, v0a, v0b, 2, 14)
    residual(lev0, f0, v0b, r0b, 4, 12)
    f1own = dot(dot(lr0, r0b[...].reshape(128, 256)), rz0[...])
    sf1[...] = f1own.reshape(4, 4, 128)
    wait_f1 = [send(sf1, rf1.at[n], a, b) for n, (a, b) in enumerate(NEAR)]

    def spread1(mine, got, cells):
        for n, (a, b) in enumerate([(0, 0)] + NEAR):
            for p in range(4):
                x, y = 4 - 4 * a + p, 4 - 4 * b
                cells[x, y : y + 4] = mine[p] if n == 0 else got[n - 1, p]

    zed1 = jnp.zeros((4, 128), F32)
    for i in range(12):
        l1[0][i, 12:16] = zed1
        f1[i, 12:16] = zed1
        u1[i, 12:16] = zed1
    for w in wait_c1:
        w.wait_recv()
    spread1(sc1, rc1, l1[0])
    for i in range(12):
        l1[0][i] = l1[0][i] * mask1(i)
    lev1 = Level(l1, 12, 16, 128, True)
    lev1.build(mask1, 1, 11)
    for w in wait_c2:
        w.wait_recv()
    for i in range(22):
        l2[0][i] = l2[0][i] * mask2(i)
    lev2 = Level(l2, 22, 24, 128, False)
    lev2.build(mask2, 2, 20)

    for w in wait_f1:
        w.wait_recv()
    spread1(sf1, rf1, f1)
    first(lev1, f1, v1a, 1, 11)
    second(lev1, f1, v1a, v1b, 2, 10)
    for p in range(4):
        su1[p] = v1b[4 + p, 4:8]
    residual(lev1, f1, v1b, r1b, 4, 8)
    sf2[...] = dot(dot(lr1, r1b[...].reshape(64, 128)), rz1[...])
    wait_f2 = [send(sf2, gf2.at[R5 - k], 0, k) for k in offs4]
    wait_u1 = [send(su1, ru1.at[n], a, b) for n, (a, b) in enumerate(NEAR)]

    for x in (0, 1):
        af2[x, 0:2] = jnp.zeros((2, 128), F32)
        af2[x, 20:24] = jnp.zeros((4, 128), F32)
    for w in wait_f2:
        w.wait_recv()
    for k in [0] + offs4:
        g = sf2[...] if k == 0 else gf2[k + R5]
        for x in (0, 1):
            af2[x, 2 * (k + R5) : 2 * (k + R5) + 2] = g[2 * x : 2 * x + 2]
    f2[10] = af2[0]
    f2[11] = af2[1]
    wait_f2 = [send(af2, f2.at[2 * (R5 - k) : 2 * (R5 - k) + 2], k, 0) for k in offs4]

    for w in wait_u1:
        w.wait_recv()
    spread1(su1, ru1, u1)
    for i in range(12):
        u1[i] = u1[i] * mask1(i)

    for w in wait_f2:
        w.wait_recv()
    mid2, pairs2 = chebyshev(COARSE_LOW, COARSE_HIGH, COARSE_STEPS)
    for i in range(2, 20):
        d = f2[i] * lev2.iv[i] * mid2
        v2a[i] = d
        d2[i] = d
    va, vb = v2a, v2b
    for m, (k2, p2) in enumerate(pairs2):
        for i in range(3 + m, 19 - m):
            r = f2[i] - lev2.apply(va, i)
            d = k2 * d2[i] + p2 * (r * lev2.iv[i])
            d2[i] = d
            vb[i] = va[i] + d
        va, vb = vb, va

    num = jnp.zeros((24, 128), F32)
    den = jnp.zeros((24, 128), F32)
    row = iota((24, 128), 0)
    own = jnp.where((row == 10) | (row == 11), mask2(10), 0.0)
    for i in range(9, 13):
        vb[i] = mask2(i)
    for i in (10, 11):
        num = num + own * (f2[i] - lev2.apply(va, i))
        den = den + own * lev2.apply(vb, i)
    sg1[0:1] = jnp.sum(num, axis=0, keepdims=True)
    sg1[1:2] = jnp.sum(den, axis=0, keepdims=True)

    def broadcast(mine, got, count, offset_of, k):
        copies = []
        for n in range(1, count):
            copy = pltpu.make_async_remote_copy(src_ref=mine, dst_ref=got.at[n - 1], send_sem=gsem.at[2 * k], recv_sem=gsem.at[2 * k + 1],
                                                device_id=dev(*offset_of(n)), device_id_type=MESH)
            copy.start()
        whole = pltpu.make_async_remote_copy(src_ref=got, dst_ref=got, send_sem=gsem.at[2 * k], recv_sem=gsem.at[2 * k + 1],
                                             device_id=dev(*offset_of(1)), device_id_type=MESH)
        whole.wait_recv()
        whole.wait_send()
        return mine[...] + jnp.sum(got[...], axis=0)

    sg2[...] = broadcast(sg1, rg1, NYD, lambda n: (0, n), 0)
    total = broadcast(sg2, rg2, NXD, lambda n: (n, 0), 1)
    num = jnp.sum(total[0:1], axis=1, keepdims=True)
    den = jnp.sum(total[1:2], axis=1, keepdims=True)
    shift = num / den
    for i in range(7, 15):
        va[i] = va[i] + shift * mask2(i)

    def post(lev, f, v, w, lo, hi, out=None):
        for i in range(lo, hi):
            w[i] = v[i] + (f[i] - lev.apply(v, i)) * lev.iv[i] * inv_mid
        for i in range(lo + 1, hi - 1):
            d = w[i] - v[i]
            r = f[i] - lev.apply(w, i)
            e = w[i] + (keep * d + push * (r * lev.iv[i]))
            if out is None:
                v[i] = e
            else:
                out[i - lo - 1] = e[4:12]

    p1 = dot(dot(lp1[...], va[7:15].reshape(192, 128)), pz1[...]).reshape(12, 16, 128)
    for i in range(12):
        u1[i] = u1[i] + p1[i]
    post(lev1, f1, u1, v1a, 1, 11)
    p0 = dot(dot(lp0[...], u1[2:10].reshape(128, 128)), pz0[...]).reshape(12, 16, 256)
    for i in range(12):
        v0b[i + 2] = v0b[i + 2] + p0[i]
    post(lev0, f0, v0b, v0a, 3, 13, o_ref)

    for w in sends:
        w.wait_send()


def solution(mesh):
    def vm(*shape):
        return pltpu.VMEM(shape, F32)

    def level(*shape):
        return [vm(*shape) for _ in range(6)]

    nsend = 4 + 8 + 2 + 10 + 8 + 10 + 8 + 8 + 8 + 8
    scratch = [
        vm(2, 2, 8, 4, 256), vm(2, 3, 8, 256), vm(2, 4, 8, 256), vm(2, 2, 8, 4, 256), vm(2, 2, 2, 4, 256), vm(2, 2, 3, 4, 256),
        vm(16, 16, 256), vm(16, 16, 256), vm(16, 16, 256), level(16, 16, 256),
        vm(4, 4, 128), vm(8, 4, 4, 128), vm(4, 4, 128), vm(8, 4, 4, 128), vm(4, 4, 128), vm(8, 4, 4, 128),
        vm(12, 16, 128), vm(12, 16, 128), vm(12, 16, 128), vm(12, 16, 128), level(12, 16, 128),
        vm(4, 128), vm(11, 4, 128), vm(2, 24, 128), vm(4, 128), vm(11, 4, 128), vm(2, 24, 128),
        vm(22, 24, 128), vm(22, 24, 128), vm(22, 24, 128), vm(22, 24, 128), level(22, 24, 128),
        vm(8, 16, 256), vm(4, 16, 128), vm(192, 192), vm(192, 128), vm(256, 128), vm(128, 128), vm(128, 128), vm(128, 256),
        vm(2, 128), vm(NYD - 1, 2, 128), vm(2, 128), vm(NXD - 1, 2, 128),
        pltpu.SemaphoreType.DMA((nsend,)), pltpu.SemaphoreType.DMA((nsend,)), pltpu.SemaphoreType.DMA((4,)),
    ]

    def body(right_side, coefficient):
        return pl.pallas_call(
            body_kernel,
            out_shape=jax.ShapeDtypeStruct((8, 8, 256), F32),
            in_specs=[pl.BlockSpec(memory_space=pltpu.VMEM)] * 2,
            out_specs=pl.BlockSpec(memory_space=pltpu.VMEM),
            scratch_shapes=scratch,
            compiler_params=pltpu.CompilerParams(collective_id=0, has_side_effects=True),
        )(right_side, coefficient)

    placed = (P("gx", "gy", None), P("gx", "gy", None))
    return jax.shard_map(body, mesh=mesh, in_specs=placed, out_specs=P("gx", "gy", None), check_vma=False)
```

```python
import jax
import jax.numpy as jnp
from jax import lax
from jax.experimental import pallas as pl
from jax.experimental.pallas import tpu as pltpu
from jax.sharding import PartitionSpec as P

SMOOTH_LOW = 0.5
SMOOTH_HIGH = 2.0
COARSE_LOW = 0.05
COARSE_HIGH = 2.0
COARSE_STEPS = 6

F32 = jnp.float32
NXD, NYD = 16, 32
NX, NY, NZ = 128, 256, 256
R5 = 5
R4 = 4
MESH = pl.DeviceIdType.MESH
NEAR = [(a, b) for a in (-1, 0, 1) for b in (-1, 0, 1) if (a, b) != (0, 0)]


def chebyshev(low_end, high_end, sweeps):
    middle = 0.5 * (high_end + low_end)
    half_span = 0.5 * (high_end - low_end)
    sig_ratio = middle / half_span
    rho_now = 1.0 / sig_ratio
    pairs = []
    for _ in range(1, sweeps):
        rho_next = 1.0 / (2.0 * sig_ratio - rho_now)
        pairs.append((rho_next * rho_now, 2.0 * rho_next / half_span))
        rho_now = rho_next
    return 1.0 / middle, pairs


def iota(shape, dim):
    return lax.broadcasted_iota(jnp.int32, shape, dim)


def dot(a, b):
    return jnp.dot(a, b, precision=lax.Precision.HIGHEST, preferred_element_type=F32)


def up1(v):
    return pltpu.roll(v, v.shape[0] - 1, 0)


def dn1(v):
    return pltpu.roll(v, 1, 0)


def lup(v):
    return pltpu.roll(v, v.shape[1] - 1, 1)


def ldn(v):
    return pltpu.roll(v, 1, 1)


def interp(out_cell, in_cell):
    home = out_cell >> 1
    near = jnp.where((out_cell & 1) == 0, home - 1, home + 1)
    return jnp.where(in_cell == home, 0.75, 0.0).astype(F32) + jnp.where(in_cell == near, 0.25, 0.0).astype(F32)


def pair_sum(fine, coarse):
    r, c = iota((fine, coarse), 0), iota((fine, coarse), 1)
    return jnp.where((r >> 1) == c, 1.0, 0.0).astype(F32)


class Level:
    def __init__(self, refs, planes, rows, lanes, zfull):
        self.c, self.wx, self.wy, self.wz, self.dg, self.iv = refs
        self.planes, self.rows, self.lanes, self.zfull = planes, rows, lanes, zfull

    def build(self, mask_of, lo, hi):
        lane = iota((self.rows, self.lanes), 1)
        c = self.c[lo - 1]
        for i in range(lo - 1, hi):
            nxt = self.c[i + 1]
            wxp = 0.5 * (c + nxt)
            self.wx[i] = wxp
            if i >= lo:
                wyp = 0.5 * (c + up1(c))
                wym = dn1(wyp)
                if self.zfull:
                    wzp = 0.5 * (c + jnp.where(lane == self.lanes - 1, 0.0, lup(c)))
                    wzm = 0.5 * (c + jnp.where(lane == 0, 0.0, ldn(c)))
                    wz = jnp.where(lane == self.lanes - 1, 0.0, wzp)
                else:
                    wzp = 0.5 * (c + lup(c))
                    wzm = ldn(wzp)
                    wz = wzp
                diag = wxp + self.wx[i - 1] + wyp + wym + wzp + wzm
                m = mask_of(i)
                self.wy[i] = wyp
                self.wz[i] = wz
                self.dg[i] = diag
                self.iv[i] = m / jnp.where(m > 0.5, diag, 1.0)
            c = nxt

    def apply(self, v, i):
        x = v[i]
        s = self.wx[i] * v[i + 1] + self.wx[i - 1] * v[i - 1]
        wy = self.wy[i]
        s = s + wy * up1(x) + dn1(wy * x)
        wz = self.wz[i]
        s = s + wz * lup(x) + ldn(wz * x)
        return self.dg[i] * x - s


def body_kernel(f_ref, c_ref, o_ref,
                sy, rxf, rxc, ry, rcf, rcc, f0, v0a, v0b, l0,
                sc1, rc1, sf1, rf1, su1, ru1, f1, u1, v1a, v1b, l1,
                sc2, gc2, ac2, rc2, sf2, gf2, af2, rf2, f2, v2a, v2b, d2, l2,
                r0b, r1b, lp1, lp0, rz0, rz1, pz1, pz0, hw, hx, y1, y0, yout,
                sg1, rg1, sg2, rg2, ssem, rsem, gsem, far):
    mx, my = lax.axis_index("gx"), lax.axis_index("gy")

    def dev(a, b):
        return (lax.rem(mx + (a + NXD), NXD), lax.rem(my + (b + NYD), NYD))

    partners = [(a, b) for a, b in NEAR if a and b]
    partners += [(0, b) for b in range(-R5, R5 + 1) if b] + [(a, 0) for a in range(-R5, R5 + 1) if a]
    barrier = pltpu.get_barrier_semaphore()
    for a, b in partners:
        pl.semaphore_signal(barrier, inc=1, device_id=dev(a, b), device_id_type=MESH)

    sends = []

    def send(src, dst, a, b):
        k = len(sends)
        copy = pltpu.make_async_remote_copy(src_ref=src, dst_ref=dst, send_sem=ssem.at[k], recv_sem=rsem.at[k],
                                            device_id=dev(a, b), device_id_type=MESH)
        copy.start()
        sends.append(copy)
        return copy

    def pack2(v):
        return v[0:2] + pltpu.roll(v[2:4], 64, 1)

    rz0[...] = pair_sum(256, 128)
    rz1[...] = pair_sum(128, 128)
    o, q = iota((16, 64), 0), iota((16, 64), 1)
    lc1 = jnp.where(((q >> 4) == (o >> 2)) & (((q & 7) >> 1) == (o & 3)), 0.125, 0.0).astype(F32)
    c1own = dot(dot(lc1, c_ref[...].reshape(64, 256)), rz0[...])
    o, q = iota((4, 16), 0), iota((4, 16), 1)
    lc2 = jnp.where(((q >> 3) == (o >> 1)) & (((q & 3) >> 1) == (o & 1)), 0.125, 0.0).astype(F32)
    sc2[...] = pack2(dot(dot(lc2, c1own), rz1[...]))
    sc1[...] = c1own.reshape(4, 4, 128)
    for p in range(8):
        fp, cp = f_ref[p], c_ref[p]
        for s in (0, 1):
            sy[s, 0, p] = fp[4 * s : 4 * s + 4]
            sy[s, 1, p] = cp[4 * s : 4 * s + 4]
    pl.semaphore_wait(barrier, len(partners))

    offs5 = [k for k in range(-R5, R5 + 1) if k]
    offs4 = [k for k in range(-R4, R4 + 1) if k]
    wait_c2 = [send(sc2, gc2.at[R5 - k], 0, k) for k in offs5]
    wait_a = []
    for sx, a in ((1, 1), (0, -1)):
        for s, b in ((1, 1), (0, -1)):
            wait_a.append(send(sy.at[s, 1, 5:8] if sx else sy.at[s, 1, 0:3], rcc.at[1 - sx, 1 - s], a, b))
            wait_a.append(send(sy.at[s, 0, 6:8] if sx else sy.at[s, 0, 0:2], rcf.at[1 - sx, 1 - s], a, b))
    for s, a in ((1, 1), (0, -1)):
        wait_a.append(send(c_ref.at[4:8] if s else c_ref.at[0:4], rxc.at[1 - s], a, 0))
        wait_a.append(send(f_ref.at[5:8] if s else f_ref.at[0:3], rxf.at[1 - s], a, 0))
    for s, b in ((1, 1), (0, -1)):
        wait_a.append(send(sy.at[s], ry.at[1 - s], 0, b))
    wait_c1 = [send(sc1, rc1.at[n], a, b) for n, (a, b) in enumerate(NEAR)]

    zed = jnp.zeros((16, 256), F32)
    for p in (0, 1, 2, 3, 12, 13, 14, 15):
        f0[p] = zed
        l0[0][p] = zed

    o, q = iota((16, 128), 0), iota((16, 128), 1)
    yr = (q & 15) - 4
    lr0 = jnp.where(((q >> 5) == (o >> 2)) & ((yr >> 1) == (o & 3)) & (yr >= 0) & (yr < 8), 0.5, 0.0).astype(F32)
    o, q = iota((4, 64), 0), iota((4, 64), 1)
    yr = (q & 15) - 4
    lr1 = jnp.where(((q >> 5) == (o >> 1)) & ((yr >> 1) == (o & 1)) & (yr >= 0) & (yr < 4), 0.5, 0.0).astype(F32)

    def prolong_matrix(planes_out, x_out0, x_in0, rows_in, planes_in, y_out0, y_in0, bx, by, nx, ny):
        shape = (planes_out * 16, planes_in * rows_in)
        r, c = iota(shape, 0), iota(shape, 1)
        xo, yo = (r >> 4) + x_out0, (r & 15) + y_out0
        if rows_in == 16:
            ci, cr = c >> 4, c & 15
        else:
            ci = (c * 2731) >> 16
            cr = c - ci * rows_in
        w = interp(xo, ci + x_in0) * interp(yo, cr + y_in0)
        gx_, gy_ = xo + mx * bx, yo + my * by
        ok = (gx_ >= 0) & (gx_ < nx) & (gy_ >= 0) & (gy_ < ny)
        return jnp.where(ok, w, 0.0)

    lp1[...] = prolong_matrix(12, -4, -3, 24, 8, -4, -10, 4, 4, 64, 128)
    lp0[...] = prolong_matrix(12, -2, -2, 16, 8, -4, -4, 8, 8, 128, 256)
    r, c = iota((128, 128), 0), iota((128, 128), 1)
    pz1[...] = jnp.where(r < 64, interp(c, r), 0.0)
    r, c = iota((128, 256), 0), iota((128, 256), 1)
    pz0[...] = interp(c, r)

    def masker(rows, lanes, halo, b, nx, ny, valid_lanes, valid_rows):
        row = iota((rows, lanes), 0)
        y = row - halo + my * b
        ok = (y >= 0) & (y < ny) & (row < valid_rows)
        if valid_lanes < lanes:
            ok = ok & (iota((rows, lanes), 1) < valid_lanes)
        base = jnp.where(ok, 1.0, 0.0).astype(F32)

        def mask_of(i):
            x = mx * b + (i - halo)
            return base * jnp.where((x >= 0) & (x < nx), 1.0, 0.0).astype(F32)

        return mask_of

    mask0 = masker(16, 256, 4, 8, NX, NY, 256, 16)
    mask1 = masker(16, 128, 4, 4, NX // 2, NY // 2, 128, 12)
    mask2 = masker(24, 128, 10, 2, NX // 4, NY // 4, 64, 22)

    def gather2(mine, got, rows, offs):
        rows[...] = jnp.zeros((24, 128), F32)
        rows[2 * R5 : 2 * R5 + 2] = mine[...]
        for k in offs:
            rows[2 * (k + R5) : 2 * (k + R5) + 2] = got[k + R5]

    def unpack2(mine, got, cells, offs, scale):
        for k in [0] + offs:
            v = mine[...] if k == 0 else got[k + R5]
            i = 2 * (k + R5)
            cells[i] = v * scale(i)
            cells[i + 1] = pltpu.roll(v, 64, 1) * scale(i + 1)

    for w in wait_c2:
        w.wait_recv()
    for b in (10, -10):
        pl.semaphore_signal(far, inc=1, device_id=dev(0, b), device_id_type=MESH)
    gather2(sc2, gc2, ac2, offs5)
    wait_c2 = [send(ac2, rc2.at[R5 - k], k, 0) for k in offs5]

    for w in wait_a:
        w.wait_recv()
    c0 = l0[0]
    for p in range(8):
        i = p + 4
        f0[i, 0:4] = ry[0, 0, p]
        f0[i, 4:12] = f_ref[p]
        f0[i, 12:16] = ry[1, 0, p]
        c0[i, 0:4] = ry[0, 1, p]
        c0[i, 4:12] = c_ref[p]
        c0[i, 12:16] = ry[1, 1, p]
    for p in range(4):
        c0[p, 4:12] = rxc[0, p]
        c0[12 + p, 4:12] = rxc[1, p]
    for p in range(3):
        f0[1 + p, 4:12] = rxf[0, p]
        f0[12 + p, 4:12] = rxf[1, p]
        for s in (0, 1):
            c0[1 + p, 12 * s : 12 * s + 4] = rcc[0, s, p]
            c0[12 + p, 12 * s : 12 * s + 4] = rcc[1, s, p]
    for p in range(2):
        for s in (0, 1):
            f0[2 + p, 12 * s : 12 * s + 4] = rcf[0, s, p]
            f0[12 + p, 12 * s : 12 * s + 4] = rcf[1, s, p]
    for i in range(16):
        c0[i] = c0[i] * mask0(i)
    lev0 = Level(l0, 16, 16, 256, True)
    lev0.build(mask0, 1, 15)

    inv_mid, ((keep, push),) = chebyshev(SMOOTH_LOW, SMOOTH_HIGH, 2)

    def first(lev, f, v, lo, hi):
        for i in range(lo, hi):
            v[i] = f[i] * lev.iv[i] * inv_mid

    def second(lev, f, va, vb, lo, hi):
        for i in range(lo, hi):
            d = va[i]
            r = f[i] - lev.apply(va, i)
            vb[i] = d + (keep * d + push * (r * lev.iv[i]))

    def residual(lev, f, v, out, lo, hi):
        for i in range(lo, hi):
            out[i - lo] = f[i] - lev.apply(v, i)

    v0a[0] = zed
    v0a[15] = zed
    first(lev0, f0, v0a, 1, 15)
    second(lev0, f0, v0a, v0b, 2, 14)
    residual(lev0, f0, v0b, r0b, 4, 12)
    f1own = dot(dot(lr0, r0b[...].reshape(128, 256)), rz0[...])
    sf1[...] = f1own.reshape(4, 4, 128)
    wait_f1 = [send(sf1, rf1.at[n], a, b) for n, (a, b) in enumerate(NEAR)]

    def spread1(mine, got, cells):
        for n, (a, b) in enumerate([(0, 0)] + NEAR):
            for p in range(4):
                x, y = 4 - 4 * a + p, 4 - 4 * b
                cells[x, y : y + 4] = mine[p] if n == 0 else got[n - 1, p]

    zed1 = jnp.zeros((4, 128), F32)
    for i in range(12):
        l1[0][i, 12:16] = zed1
        f1[i, 12:16] = zed1
        u1[i, 12:16] = zed1
    for w in wait_c1:
        w.wait_recv()
    spread1(sc1, rc1, l1[0])
    for i in range(12):
        l1[0][i] = l1[0][i] * mask1(i)
    lev1 = Level(l1, 12, 16, 128, True)
    lev1.build(mask1, 1, 11)
    for w in wait_c2:
        w.wait_recv()
    unpack2(ac2, rc2, l2[0], offs5, mask2)
    lev2 = Level(l2, 22, 24, 128, False)
    lev2.build(mask2, 2, 20)

    def rhs(lev, f, v, i):
        return -lev.apply(v, i) if f is None else f[i] - lev.apply(v, i)

    def post(lev, f, v, w, lo, hi, out=None):
        for i in range(lo, hi):
            w[i] = v[i] + rhs(lev, f, v, i) * lev.iv[i] * inv_mid
        for i in range(lo + 1, hi - 1):
            d = w[i] - v[i]
            e = w[i] + (keep * d + push * (rhs(lev, f, w, i) * lev.iv[i]))
            if out is None:
                v[i] = e
            else:
                out[i - lo - 1] = e[4:12]

    mid2, pairs2 = chebyshev(COARSE_LOW, COARSE_HIGH, COARSE_STEPS)
    row = iota((24, 128), 0)
    own = jnp.where((row == 10) | (row == 11), 1.0, 0.0).astype(F32)
    for i in range(3, 19):
        v2a[i] = mask2(i)
    y1[...] = dot(dot(lp1[...], v2a[7:15].reshape(192, 128)), pz1[...]).reshape(12, 16, 128)
    den = jnp.zeros((24, 128), F32)
    va, vb = v2a, v2b
    for m, (k2, p2) in enumerate([(0.0, mid2)] + pairs2):
        for i in range(4 + m, 18 - m):
            r = lev2.apply(va, i)
            if m == 0 and i in (10, 11):
                den = den + own * mask2(i) * r
            d = -p2 * (r * lev2.iv[i])
            if m:
                d = k2 * d2[i] + d
            d2[i] = d
            vb[i] = va[i] + d
        va, vb = vb, va
    r, c = iota((128, 96), 0), iota((128, 96), 1)
    ci = (c * 2731) >> 16
    spread = ((((r >> 4) - 2) >> 1) == ci - 1) & ((((r & 15) - 4) >> 1) == c - ci * 24 - 10)
    spread = jnp.where(spread, 0.5, 0.0).astype(F32)
    r, c = iota((128, 128), 0), iota((128, 128), 1)
    hw[2:10] = dot(dot(spread, va[9:13].reshape(96, 128)), jnp.where((c >> 1) == r, 1.0, 0.0).astype(F32)).reshape(8, 16, 128)
    post(lev1, None, hw, hx, 3, 9)
    num = jnp.zeros((4, 128), F32)
    for p in range(4):
        num = num + hw[4 + p, 4:8] * sf1[p]
    sg1[0:1] = jnp.sum(num, axis=0, keepdims=True)
    sg1[1:2] = jnp.sum(den, axis=0, keepdims=True)

    def broadcast(mine, got, count, offset_of, k):
        for n in range(1, count):
            copy = pltpu.make_async_remote_copy(src_ref=mine, dst_ref=got.at[n - 1], send_sem=gsem.at[2 * k], recv_sem=gsem.at[2 * k + 1],
                                                device_id=dev(*offset_of(n)), device_id_type=MESH)
            copy.start()
        return pltpu.make_async_remote_copy(src_ref=got, dst_ref=got, send_sem=gsem.at[2 * k], recv_sem=gsem.at[2 * k + 1],
                                            device_id=dev(*offset_of(1)), device_id_type=MESH)

    pl.semaphore_wait(far, 2)
    all_y = broadcast(sg1, rg1, NYD, lambda n: (0, n), 0)

    for w in wait_f1:
        w.wait_recv()
    spread1(sf1, rf1, f1)
    first(lev1, f1, v1a, 1, 11)
    second(lev1, f1, v1a, v1b, 2, 10)
    residual(lev1, f1, v1b, r1b, 4, 8)
    sf2[...] = pack2(dot(dot(lr1, r1b[...].reshape(64, 128)), rz1[...]))
    wait_f2 = [send(sf2, gf2.at[R5 - k], 0, k) for k in offs4]
    for p in range(4):
        su1[p] = v1b[4 + p, 4:8]
    wait_u1 = [send(su1, ru1.at[n], a, b) for n, (a, b) in enumerate(NEAR)]

    post(lev1, None, y1, v1a, 1, 11)
    y0[2:14] = dot(dot(lp0[...], y1[2:10].reshape(128, 128)), pz0[...]).reshape(12, 16, 256)
    post(lev0, None, y0, v0a, 3, 13, yout)

    for w in wait_f2:
        w.wait_recv()
    gather2(sf2, gf2, af2, offs4)
    wait_f2 = [send(af2, rf2.at[R5 - k], k, 0) for k in offs4]

    for w in wait_u1:
        w.wait_recv()
    spread1(su1, ru1, u1)
    for i in range(12):
        u1[i] = u1[i] * mask1(i)

    all_y.wait_recv()
    sg2[...] = sg1[...] + jnp.sum(rg1[...], axis=0)
    all_x = broadcast(sg2, rg2, NXD, lambda n: (n, 0), 1)

    for w in wait_f2:
        w.wait_recv()
    unpack2(af2, rf2, f2, offs4, mask2)
    for i in range(2, 20):
        d = f2[i] * lev2.iv[i] * mid2
        v2a[i] = d
        d2[i] = d
    va, vb = v2a, v2b
    for m, (k2, p2) in enumerate(pairs2):
        for i in range(3 + m, 19 - m):
            r = f2[i] - lev2.apply(va, i)
            d = k2 * d2[i] + p2 * (r * lev2.iv[i])
            d2[i] = d
            vb[i] = va[i] + d
        va, vb = vb, va

    p1 = dot(dot(lp1[...], va[7:15].reshape(192, 128)), pz1[...]).reshape(12, 16, 128)
    for i in range(12):
        u1[i] = u1[i] + p1[i]
    post(lev1, f1, u1, v1a, 1, 11)
    p0 = dot(dot(lp0[...], u1[2:10].reshape(128, 128)), pz0[...]).reshape(12, 16, 256)
    for i in range(12):
        v0b[i + 2] = v0b[i + 2] + p0[i]
    post(lev0, f0, v0b, v0a, 3, 13, o_ref)

    all_x.wait_recv()
    total = sg2[...] + jnp.sum(rg2[...], axis=0)
    shift = jnp.sum(total[0:1], axis=1, keepdims=True) / jnp.sum(total[1:2], axis=1, keepdims=True)
    for p in range(8):
        o_ref[p] = o_ref[p] + shift * yout[p]
    all_y.wait_send()
    all_x.wait_send()

    for w in sends:
        w.wait_send()


def solution(mesh):
    def vm(*shape):
        return pltpu.VMEM(shape, F32)

    def level(*shape):
        return [vm(*shape) for _ in range(6)]

    nsend = 4 + 8 + 2 + 10 + 8 + 10 + 8 + 8 + 8 + 8
    scratch = [
        vm(2, 2, 8, 4, 256), vm(2, 3, 8, 256), vm(2, 4, 8, 256), vm(2, 2, 8, 4, 256), vm(2, 2, 2, 4, 256), vm(2, 2, 3, 4, 256),
        vm(16, 16, 256), vm(16, 16, 256), vm(16, 16, 256), level(16, 16, 256),
        vm(4, 4, 128), vm(8, 4, 4, 128), vm(4, 4, 128), vm(8, 4, 4, 128), vm(4, 4, 128), vm(8, 4, 4, 128),
        vm(12, 16, 128), vm(12, 16, 128), vm(12, 16, 128), vm(12, 16, 128), level(12, 16, 128),
        vm(2, 128), vm(11, 2, 128), vm(24, 128), vm(11, 24, 128), vm(2, 128), vm(11, 2, 128), vm(24, 128), vm(11, 24, 128),
        vm(22, 24, 128), vm(22, 24, 128), vm(22, 24, 128), vm(22, 24, 128), level(22, 24, 128),
        vm(8, 16, 256), vm(4, 16, 128), vm(192, 192), vm(192, 128), vm(256, 128), vm(128, 128), vm(128, 128), vm(128, 256),
        vm(12, 16, 128), vm(12, 16, 128), vm(12, 16, 128), vm(16, 16, 256), vm(8, 8, 256),
        vm(2, 128), vm(NYD - 1, 2, 128), vm(2, 128), vm(NXD - 1, 2, 128),
        pltpu.SemaphoreType.DMA((nsend,)), pltpu.SemaphoreType.DMA((nsend,)), pltpu.SemaphoreType.DMA((4,)), pltpu.SemaphoreType.REGULAR,
    ]

    def body(right_side, coefficient):
        return pl.pallas_call(
            body_kernel,
            out_shape=jax.ShapeDtypeStruct((8, 8, 256), F32),
            in_specs=[pl.BlockSpec(memory_space=pltpu.VMEM)] * 2,
            out_specs=pl.BlockSpec(memory_space=pltpu.VMEM),
            scratch_shapes=scratch,
            compiler_params=pltpu.CompilerParams(collective_id=0, has_side_effects=True),
        )(right_side, coefficient)

    placed = (P("gx", "gy", None), P("gx", "gy", None))
    return jax.shard_map(body, mesh=mesh, in_specs=placed, out_specs=P("gx", "gy", None), check_vma=False)
```

```python
import jax
import jax.numpy as jnp
from jax import lax
from jax.experimental import pallas as pl
from jax.experimental.pallas import tpu as pltpu
from jax.sharding import PartitionSpec as P

SMOOTH_LOW = 0.5
SMOOTH_HIGH = 2.0
COARSE_LOW = 0.05
COARSE_HIGH = 2.0
COARSE_STEPS = 6

F32 = jnp.float32
NXD, NYD = 16, 32
NX, NY, NZ = 128, 256, 256
R2 = 4
H2 = 2 * R2
MESH = pl.DeviceIdType.MESH
NEAR = [(a, b) for a in (-1, 0, 1) for b in (-1, 0, 1) if (a, b) != (0, 0)]


def chebyshev(low_end, high_end, sweeps):
    middle = 0.5 * (high_end + low_end)
    half_span = 0.5 * (high_end - low_end)
    sig_ratio = middle / half_span
    rho_now = 1.0 / sig_ratio
    pairs = []
    for _ in range(1, sweeps):
        rho_next = 1.0 / (2.0 * sig_ratio - rho_now)
        pairs.append((rho_next * rho_now, 2.0 * rho_next / half_span))
        rho_now = rho_next
    return 1.0 / middle, pairs


def iota(shape, dim):
    return lax.broadcasted_iota(jnp.int32, shape, dim)


def dot(a, b):
    return jnp.dot(a, b, precision=lax.Precision.HIGHEST, preferred_element_type=F32)


def up1(v):
    return pltpu.roll(v, v.shape[0] - 1, 0)


def dn1(v):
    return pltpu.roll(v, 1, 0)


def lup(v):
    return pltpu.roll(v, v.shape[1] - 1, 1)


def ldn(v):
    return pltpu.roll(v, 1, 1)


def interp(out_cell, in_cell):
    home = out_cell >> 1
    near = jnp.where((out_cell & 1) == 0, home - 1, home + 1)
    return jnp.where(in_cell == home, 0.75, 0.0).astype(F32) + jnp.where(in_cell == near, 0.25, 0.0).astype(F32)


def pair_sum(fine, coarse):
    r, c = iota((fine, coarse), 0), iota((fine, coarse), 1)
    return jnp.where((r >> 1) == c, 1.0, 0.0).astype(F32)


class Level:
    def __init__(self, refs, planes, rows, lanes, zfull):
        self.c, self.wx, self.wy, self.wz, self.dg, self.iv = refs
        self.planes, self.rows, self.lanes, self.zfull = planes, rows, lanes, zfull

    def build(self, mask_of, lo, hi):
        lane = iota((self.rows, self.lanes), 1)
        c = self.c[lo - 1]
        for i in range(lo - 1, hi):
            nxt = self.c[i + 1]
            wxp = 0.5 * (c + nxt)
            self.wx[i] = wxp
            if i >= lo:
                wyp = 0.5 * (c + up1(c))
                wym = dn1(wyp)
                if self.zfull:
                    wzp = 0.5 * (c + jnp.where(lane == self.lanes - 1, 0.0, lup(c)))
                    wzm = 0.5 * (c + jnp.where(lane == 0, 0.0, ldn(c)))
                    wz = jnp.where(lane == self.lanes - 1, 0.0, wzp)
                else:
                    wzp = 0.5 * (c + lup(c))
                    wzm = ldn(wzp)
                    wz = wzp
                diag = wxp + self.wx[i - 1] + wyp + wym + wzp + wzm
                m = mask_of(i)
                self.wy[i] = wyp
                self.wz[i] = wz
                self.dg[i] = diag
                self.iv[i] = m / jnp.where(diag > 0.0, diag, 1.0)
            c = nxt

    def apply(self, v, i):
        x = v[i]
        s = self.wx[i] * v[i + 1] + self.wx[i - 1] * v[i - 1]
        wy = self.wy[i]
        s = s + wy * up1(x) + dn1(wy * x)
        wz = self.wz[i]
        s = s + wz * lup(x) + ldn(wz * x)
        return self.dg[i] * x - s


def body_kernel(f_hbm, c_hbm, o_ref,
                f_ref, c_ref, sy, sc, rxf, rxc, ry, rc, sux, suy, rux, ruy, ruc, f0, v0a, v0b, l0,
                sc1, rc1, sf1, rf1, su1, ru1, f1, u1, v1a, v1b, l1,
                sc2, gc2, ac2, rc2, sf2, gf2, af2, rf2, f2, v2a, v2b, d2, l2,
                r0b, r1b, lp1, lp0, rz0, rz1, pz1, pz0, hw, hx, y1, y0, yout,
                sg1, rg1, sg2, rg2, ssem, rsem, gsem, far):
    mx, my = lax.axis_index("gx"), lax.axis_index("gy")

    def dev(a, b):
        return (lax.rem(mx + (a + NXD), NXD), lax.rem(my + (b + NYD), NYD))

    partners = [(a, b) for a, b in NEAR if a and b]
    partners += [(0, b) for b in range(-R2, R2 + 1) if b] + [(a, 0) for a in range(-R2, R2 + 1) if a]
    barrier = pltpu.get_barrier_semaphore()
    for a, b in partners:
        pl.semaphore_signal(barrier, inc=1, device_id=dev(a, b), device_id_type=MESH)

    get_c = pltpu.make_async_copy(c_hbm, c_ref, gsem.at[4])
    get_f = pltpu.make_async_copy(f_hbm, f_ref, gsem.at[5])
    get_c.start()
    get_f.start()
    sends = []

    def send(src, dst, a, b):
        k = len(sends)
        copy = pltpu.make_async_remote_copy(src_ref=src, dst_ref=dst, send_sem=ssem.at[k], recv_sem=rsem.at[k],
                                            device_id=dev(a, b), device_id_type=MESH)
        copy.start()
        sends.append(copy)
        return copy

    def pack2(v):
        return v[0:2] + pltpu.roll(v[2:4], 64, 1)

    rz0[...] = pair_sum(256, 128)
    rz1[...] = pair_sum(128, 128)
    o, q = iota((16, 64), 0), iota((16, 64), 1)
    lc1 = jnp.where(((q >> 4) == (o >> 2)) & (((q & 7) >> 1) == (o & 3)), 0.125, 0.0).astype(F32)
    get_c.wait()
    c1own = dot(dot(lc1, c_ref[...].reshape(64, 256)), rz0[...])
    o, q = iota((4, 16), 0), iota((4, 16), 1)
    lc2 = jnp.where(((q >> 3) == (o >> 1)) & (((q & 3) >> 1) == (o & 1)), 0.125, 0.0).astype(F32)
    sc2[...] = pack2(dot(dot(lc2, c1own), rz1[...]))
    sc1[...] = c1own.reshape(4, 4, 128)
    get_f.wait()
    for p in range(8):
        fp, cp = f_ref[p], c_ref[p]
        for s in (0, 1):
            sy[s, 0, p] = fp[4 * s : 4 * s + 4]
            sy[s, 1, p] = cp[4 * s : 4 * s + 4]
    for sx in (0, 1):
        for s in (0, 1):
            sc[sx, s, 0] = c_ref[6 * sx, 6 * s : 6 * s + 2]
            sc[sx, s, 1] = c_ref[6 * sx + 1, 6 * s : 6 * s + 2]
            sc[sx, s, 2] = f_ref[7 * sx, 6 * s : 6 * s + 2]
    pl.semaphore_wait(barrier, len(partners))

    offs = [k for k in range(-R2, R2 + 1) if k]
    wait_c2 = [send(sc2, gc2.at[R2 - k], 0, k) for k in offs]
    wait_a = []
    for sx, a in ((1, 1), (0, -1)):
        for s, b in ((1, 1), (0, -1)):
            wait_a.append(send(sc.at[sx, s], rc.at[1 - sx, 1 - s], a, b))
    for s, a in ((1, 1), (0, -1)):
        wait_a.append(send(c_ref.at[5:8] if s else c_ref.at[0:3], rxc.at[1 - s], a, 0))
        wait_a.append(send(f_ref.at[6:8] if s else f_ref.at[0:2], rxf.at[1 - s], a, 0))
    for s, b in ((1, 1), (0, -1)):
        wait_a.append(send(sy.at[s], ry.at[1 - s], 0, b))
    wait_c1 = [send(sc1, rc1.at[n], a, b) for n, (a, b) in enumerate(NEAR)]

    zed = jnp.zeros((16, 256), F32)
    for p in (0, 1, 2, 3, 12, 13, 14, 15):
        f0[p] = zed
        l0[0][p] = zed

    o, q = iota((16, 128), 0), iota((16, 128), 1)
    yr = (q & 15) - 4
    lr0 = jnp.where(((q >> 5) == (o >> 2)) & ((yr >> 1) == (o & 3)) & (yr >= 0) & (yr < 8), 0.5, 0.0).astype(F32)
    o, q = iota((4, 64), 0), iota((4, 64), 1)
    yr = (q & 15) - 4
    lr1 = jnp.where(((q >> 5) == (o >> 1)) & ((yr >> 1) == (o & 1)) & (yr >= 0) & (yr < 4), 0.5, 0.0).astype(F32)

    def prolong_matrix(planes_out, x_out0, x_in0, rows_in, planes_in, y_out0, y_in0, bx, by, nx, ny):
        shape = (planes_out * 16, planes_in * rows_in)
        r, c = iota(shape, 0), iota(shape, 1)
        xo, yo = (r >> 4) + x_out0, (r & 15) + y_out0
        if rows_in == 16:
            ci, cr = c >> 4, c & 15
        else:
            ci = (c * 2731) >> 16
            cr = c - ci * rows_in
        w = interp(xo, ci + x_in0) * interp(yo, cr + y_in0)
        gx_, gy_ = xo + mx * bx, yo + my * by
        ok = (gx_ >= 0) & (gx_ < nx) & (gy_ >= 0) & (gy_ < ny)
        return jnp.where(ok, w, 0.0)

    lp1[...] = prolong_matrix(12, -4, -3, 24, 8, -4, -H2, 4, 4, 64, 128)
    lp0[...] = prolong_matrix(12, -2, -2, 16, 8, -4, -4, 8, 8, 128, 256)
    r, c = iota((128, 128), 0), iota((128, 128), 1)
    pz1[...] = jnp.where(r < 64, interp(c, r), 0.0)
    r, c = iota((128, 256), 0), iota((128, 256), 1)
    pz0[...] = interp(c, r)

    def masker(rows, lanes, halo, b, nx, ny, valid_lanes, valid_rows):
        row = iota((rows, lanes), 0)
        y = row - halo + my * b
        ok = (y >= 0) & (y < ny) & (row < valid_rows)
        if valid_lanes < lanes:
            ok = ok & (iota((rows, lanes), 1) < valid_lanes)
        base = jnp.where(ok, 1.0, 0.0).astype(F32)

        def mask_of(i):
            x = mx * b + (i - halo)
            return base * jnp.where((x >= 0) & (x < nx), 1.0, 0.0).astype(F32)

        return mask_of

    mask0 = masker(16, 256, 4, 8, NX, NY, 256, 16)
    mask1 = masker(16, 128, 4, 4, NX // 2, NY // 2, 128, 12)
    mask2 = masker(24, 128, H2, 2, NX // 4, NY // 4, 64, 2 * H2 + 2)

    def gather2(mine, got, rows):
        rows[...] = jnp.zeros((24, 128), F32)
        rows[H2 : H2 + 2] = mine[...]
        for k in offs:
            rows[2 * (k + R2) : 2 * (k + R2) + 2] = got[k + R2]

    def unpack2(mine, got, cells):
        for k in [0] + offs:
            v = mine[...] if k == 0 else got[k + R2]
            i = 2 * (k + R2)
            cells[i] = v * mask2(i)
            cells[i + 1] = pltpu.roll(v, 64, 1) * mask2(i + 1)

    def spread1(mine, got, cells):
        for n, (a, b) in enumerate([(0, 0)] + NEAR):
            for p in range(4):
                x, y = 4 - 4 * a + p, 4 - 4 * b
                cells[x, y : y + 4] = mine[p] if n == 0 else got[n - 1, p]

    for w in wait_c2:
        w.wait_recv()
    for b in (8, -8):
        pl.semaphore_signal(far, inc=1, device_id=dev(0, b), device_id_type=MESH)
    gather2(sc2, gc2, ac2)
    wait_c2 = [send(ac2, rc2.at[R2 - k], k, 0) for k in offs]

    zed1 = jnp.zeros((4, 128), F32)
    for i in range(12):
        l1[0][i, 12:16] = zed1
        f1[i, 12:16] = zed1
        u1[i, 12:16] = zed1
    for w in wait_c1:
        w.wait_recv()
    spread1(sc1, rc1, l1[0])
    for i in range(12):
        l1[0][i] = l1[0][i] * mask1(i)
    lev1 = Level(l1, 12, 16, 128, True)
    lev1.build(mask1, 1, 11)

    for w in wait_a:
        w.wait_recv()
    c0 = l0[0]
    for p in range(8):
        i = p + 4
        f0[i, 0:4] = ry[0, 0, p]
        f0[i, 4:12] = f_ref[p]
        f0[i, 12:16] = ry[1, 0, p]
        c0[i, 0:4] = ry[0, 1, p]
        c0[i, 4:12] = c_ref[p]
        c0[i, 12:16] = ry[1, 1, p]
    for p in range(3):
        c0[1 + p, 4:12] = rxc[0, p]
        c0[12 + p, 4:12] = rxc[1, p]
    for p in range(2):
        f0[2 + p, 4:12] = rxf[0, p]
        f0[12 + p, 4:12] = rxf[1, p]
        for s in (0, 1):
            c0[2 + p, 2 + 10 * s : 4 + 10 * s] = rc[0, s, p]
            c0[12 + p, 2 + 10 * s : 4 + 10 * s] = rc[1, s, p]
    for s in (0, 1):
        f0[3, 2 + 10 * s : 4 + 10 * s] = rc[0, s, 2]
        f0[12, 2 + 10 * s : 4 + 10 * s] = rc[1, s, 2]
    for i in range(16):
        c0[i] = c0[i] * mask0(i)
    lev0 = Level(l0, 16, 16, 256, True)
    lev0.build(mask0, 2, 14)

    inv_mid, ((keep, push),) = chebyshev(SMOOTH_LOW, SMOOTH_HIGH, 2)

    def first(lev, f, v, lo, hi):
        for i in range(lo, hi):
            v[i] = f[i] * lev.iv[i] * inv_mid

    def second(lev, f, va, vb, lo, hi):
        for i in range(lo, hi):
            d = va[i]
            r = f[i] - lev.apply(va, i)
            vb[i] = d + (keep * d + push * (r * lev.iv[i]))

    def residual(lev, f, v, out, lo, hi):
        for i in range(lo, hi):
            out[i - lo] = f[i] - lev.apply(v, i)

    first(lev0, f0, v0a, 2, 14)
    second(lev0, f0, v0a, v0b, 3, 13)
    residual(lev0, f0, v0b, r0b, 4, 12)
    f1own = dot(dot(lr0, r0b[...].reshape(128, 256)), rz0[...])
    sf1[...] = f1own.reshape(4, 4, 128)
    wait_f1 = [send(sf1, rf1.at[n], a, b) for n, (a, b) in enumerate(NEAR)]

    for p in range(8):
        for s in (0, 1):
            suy[s, p] = v0b[4 + p, 4 + 6 * s : 6 + 6 * s]
    for p in range(2):
        for s in (0, 1):
            sux[s, p] = v0b[4 + 6 * s + p, 4:12]
    wait_u0 = []
    for sx, a in ((1, 1), (0, -1)):
        for s, b in ((1, 1), (0, -1)):
            wait_u0.append(send(suy.at[s, 7 * sx], ruc.at[1 - sx, 1 - s], a, b))
    wait_u0 += [send(sux.at[s], rux.at[1 - s], a, 0) for s, a in ((1, 1), (0, -1))]
    wait_u0 += [send(suy.at[s], ruy.at[1 - s], 0, b) for s, b in ((1, 1), (0, -1))]

    for w in wait_c2:
        w.wait_recv()
    unpack2(ac2, rc2, l2[0])
    lev2 = Level(l2, 18, 24, 128, False)
    lev2.build(mask2, 1, 17)

    def rhs(lev, f, v, i):
        return -lev.apply(v, i) if f is None else f[i] - lev.apply(v, i)

    def post(lev, f, v, w, lo, hi, out=None):
        for i in range(lo, hi):
            w[i] = v[i] + rhs(lev, f, v, i) * lev.iv[i] * inv_mid
        for i in range(lo + 1, hi - 1):
            d = w[i] - v[i]
            e = w[i] + (keep * d + push * (rhs(lev, f, w, i) * lev.iv[i]))
            if out is None:
                v[i] = e
            else:
                out[i - lo - 1] = e[4:12]

    mid2, pairs2 = chebyshev(COARSE_LOW, COARSE_HIGH, COARSE_STEPS)
    row = iota((24, 128), 0)
    own = jnp.where((row == H2) | (row == H2 + 1), 1.0, 0.0).astype(F32)
    for i in range(1, 17):
        v2a[i] = mask2(i)
    y1[...] = dot(dot(lp1[...], v2a[5:13].reshape(192, 128)), pz1[...]).reshape(12, 16, 128)
    den = jnp.zeros((24, 128), F32)
    va, vb = v2a, v2b
    for m, (k2, p2) in enumerate([(0.0, mid2)] + pairs2):
        for i in range(2 + m, 16 - m):
            r = lev2.apply(va, i)
            if m == 0 and i in (H2, H2 + 1):
                den = den + own * mask2(i) * r
            d = -p2 * (r * lev2.iv[i])
            if m:
                d = k2 * d2[i] + d
            d2[i] = d
            vb[i] = va[i] + d
        va, vb = vb, va
    r, c = iota((128, 96), 0), iota((128, 96), 1)
    ci = (c * 2731) >> 16
    spread = ((((r >> 4) - 2) >> 1) == ci - 1) & ((((r & 15) - 4) >> 1) == c - ci * 24 - H2)
    spread = jnp.where(spread, 0.5, 0.0).astype(F32)
    r, c = iota((128, 128), 0), iota((128, 128), 1)
    hw[2:10] = dot(dot(spread, va[7:11].reshape(96, 128)), jnp.where((c >> 1) == r, 1.0, 0.0).astype(F32)).reshape(8, 16, 128)
    post(lev1, None, hw, hx, 3, 9)
    num = jnp.zeros((4, 128), F32)
    for p in range(4):
        num = num + hw[4 + p, 4:8] * sf1[p]
    sg1[0:1] = jnp.sum(num, axis=0, keepdims=True)
    sg1[1:2] = jnp.sum(den, axis=0, keepdims=True)

    def broadcast(mine, got, count, offset_of, k):
        for n in range(1, count):
            copy = pltpu.make_async_remote_copy(src_ref=mine, dst_ref=got.at[n - 1], send_sem=gsem.at[2 * k], recv_sem=gsem.at[2 * k + 1],
                                                device_id=dev(*offset_of(n)), device_id_type=MESH)
            copy.start()
        return pltpu.make_async_remote_copy(src_ref=got, dst_ref=got, send_sem=gsem.at[2 * k], recv_sem=gsem.at[2 * k + 1],
                                            device_id=dev(*offset_of(1)), device_id_type=MESH)

    pl.semaphore_wait(far, 2)
    all_y = broadcast(sg1, rg1, NYD, lambda n: (0, n), 0)

    for w in wait_f1:
        w.wait_recv()
    spread1(sf1, rf1, f1)
    first(lev1, f1, v1a, 1, 11)
    second(lev1, f1, v1a, v1b, 2, 10)
    residual(lev1, f1, v1b, r1b, 4, 8)
    f2own = dot(dot(lr1, r1b[...].reshape(64, 128)), rz1[...])
    g0 = f2own[0:2] * lev2.iv[H2, H2 : H2 + 2] * mid2
    g1 = f2own[2:4] * lev2.iv[H2 + 1, H2 : H2 + 2] * mid2
    sf2[...] = g0 + pltpu.roll(g1, 64, 1)
    wait_f2 = [send(sf2, gf2.at[R2 - k], 0, k) for k in offs]
    for p in range(4):
        su1[p] = v1b[4 + p, 4:8]
    wait_u1 = [send(su1, ru1.at[n], a, b) for n, (a, b) in enumerate(NEAR)]

    post(lev1, None, y1, v1a, 1, 11)
    y0[2:14] = dot(dot(lp0[...], y1[2:10].reshape(128, 128)), pz0[...]).reshape(12, 16, 256)
    post(lev0, None, y0, v0a, 3, 13, yout)

    for w in wait_f2:
        w.wait_recv()
    gather2(sf2, gf2, af2)
    wait_f2 = [send(af2, rf2.at[R2 - k], k, 0) for k in offs]

    for w in wait_u1:
        w.wait_recv()
    spread1(su1, ru1, u1)
    for i in range(12):
        u1[i] = u1[i] * mask1(i)

    for w in wait_u0:
        w.wait_recv()
    for p in range(8):
        v0b[4 + p, 2:4] = ruy[0, p]
        v0b[4 + p, 12:14] = ruy[1, p]
    for i in (2, 3, 12, 13):
        v0b[i] = zed
    for p in range(2):
        v0b[2 + p, 4:12] = rux[0, p]
        v0b[12 + p, 4:12] = rux[1, p]
    for s in (0, 1):
        v0b[3, 2 + 10 * s : 4 + 10 * s] = ruc[0, s]
        v0b[12, 2 + 10 * s : 4 + 10 * s] = ruc[1, s]
    for i in range(2, 14):
        v0b[i] = v0b[i] * mask0(i)

    all_y.wait_recv()
    sg2[...] = sg1[...] + jnp.sum(rg1[...], axis=0)
    all_x = broadcast(sg2, rg2, NXD, lambda n: (n, 0), 1)

    for w in wait_f2:
        w.wait_recv()
    unpack2(af2, rf2, v2a)
    for i in range(1, 17):
        d = v2a[i]
        d2[i] = d
        f2[i] = d * (lev2.dg[i] * (1.0 / mid2))
    va, vb = v2a, v2b
    for m, (k2, p2) in enumerate(pairs2):
        for i in range(1 + m, 17 - m):
            r = f2[i] - lev2.apply(va, i)
            d = k2 * d2[i] + p2 * (r * lev2.iv[i])
            d2[i] = d
            vb[i] = va[i] + d
        va, vb = vb, va

    p1 = dot(dot(lp1[...], va[5:13].reshape(192, 128)), pz1[...]).reshape(12, 16, 128)
    for i in range(12):
        u1[i] = u1[i] + p1[i]
    post(lev1, f1, u1, v1a, 1, 11)
    p0 = dot(dot(lp0[...], u1[2:10].reshape(128, 128)), pz0[...]).reshape(12, 16, 256)
    for i in range(12):
        v0b[i + 2] = v0b[i + 2] + p0[i]
    post(lev0, f0, v0b, v0a, 3, 13, o_ref)

    all_x.wait_recv()
    total = sg2[...] + jnp.sum(rg2[...], axis=0)
    shift = jnp.sum(total[0:1], axis=1, keepdims=True) / jnp.sum(total[1:2], axis=1, keepdims=True)
    for p in range(8):
        o_ref[p] = o_ref[p] + shift * yout[p]
    all_y.wait_send()
    all_x.wait_send()

    for w in sends:
        w.wait_send()


def solution(mesh):
    def vm(*shape):
        return pltpu.VMEM(shape, F32)

    def level(*shape):
        return [vm(*shape) for _ in range(6)]

    nsend = 4 + 4 + 2 + 8 + 8 + 8 + 8 + 8 + 8 + 8 + 8
    scratch = [
        vm(8, 8, 256), vm(8, 8, 256), vm(2, 2, 8, 4, 256), vm(2, 2, 3, 2, 256), vm(2, 2, 8, 256), vm(2, 3, 8, 256), vm(2, 2, 8, 4, 256),
        vm(2, 2, 3, 2, 256), vm(2, 2, 8, 256), vm(2, 8, 2, 256), vm(2, 2, 8, 256), vm(2, 8, 2, 256), vm(2, 2, 2, 256),
        vm(16, 16, 256), vm(16, 16, 256), vm(16, 16, 256), level(16, 16, 256),
        vm(4, 4, 128), vm(8, 4, 4, 128), vm(4, 4, 128), vm(8, 4, 4, 128), vm(4, 4, 128), vm(8, 4, 4, 128),
        vm(12, 16, 128), vm(12, 16, 128), vm(12, 16, 128), vm(12, 16, 128), level(12, 16, 128),
        vm(2, 128), vm(9, 2, 128), vm(24, 128), vm(9, 24, 128), vm(2, 128), vm(9, 2, 128), vm(24, 128), vm(9, 24, 128),
        vm(18, 24, 128), vm(18, 24, 128), vm(18, 24, 128), vm(18, 24, 128), level(18, 24, 128),
        vm(8, 16, 256), vm(4, 16, 128), vm(192, 192), vm(192, 128), vm(256, 128), vm(128, 128), vm(128, 128), vm(128, 256),
        vm(12, 16, 128), vm(12, 16, 128), vm(12, 16, 128), vm(16, 16, 256), vm(8, 8, 256),
        vm(2, 128), vm(NYD - 1, 2, 128), vm(2, 128), vm(NXD - 1, 2, 128),
        pltpu.SemaphoreType.DMA((nsend,)), pltpu.SemaphoreType.DMA((nsend,)), pltpu.SemaphoreType.DMA((6,)), pltpu.SemaphoreType.REGULAR,
    ]

    def body(right_side, coefficient):
        return pl.pallas_call(
            body_kernel,
            out_shape=jax.ShapeDtypeStruct((8, 8, 256), F32),
            in_specs=[pl.BlockSpec(memory_space=pl.ANY)] * 2,
            out_specs=pl.BlockSpec(memory_space=pltpu.VMEM),
            scratch_shapes=scratch,
            compiler_params=pltpu.CompilerParams(collective_id=0, has_side_effects=True),
        )(right_side, coefficient)

    placed = (P("gx", "gy", None), P("gx", "gy", None))
    return jax.shard_map(body, mesh=mesh, in_specs=placed, out_specs=P("gx", "gy", None), check_vma=False)
```

```python
import jax
import jax.numpy as jnp
from jax import lax
from jax.experimental import pallas as pl
from jax.experimental.pallas import tpu as pltpu
from jax.sharding import PartitionSpec as P

SMOOTH_LOW = 0.5
SMOOTH_HIGH = 2.0
COARSE_LOW = 0.05
COARSE_HIGH = 2.0
COARSE_STEPS = 6

F32 = jnp.float32
NXD, NYD = 16, 32
NX, NY, NZ = 128, 256, 256
R2 = 4
H2 = 2 * R2
MESH = pl.DeviceIdType.MESH
NEAR = [(1, 1), (1, -1), (-1, 1), (-1, -1), (1, 0), (-1, 0), (0, 1), (0, -1)]


def chebyshev(low_end, high_end, sweeps):
    middle = 0.5 * (high_end + low_end)
    half_span = 0.5 * (high_end - low_end)
    sig_ratio = middle / half_span
    rho_now = 1.0 / sig_ratio
    pairs = []
    for _ in range(1, sweeps):
        rho_next = 1.0 / (2.0 * sig_ratio - rho_now)
        pairs.append((rho_next * rho_now, 2.0 * rho_next / half_span))
        rho_now = rho_next
    return 1.0 / middle, pairs


def iota(shape, dim):
    return lax.broadcasted_iota(jnp.int32, shape, dim)


def thirds(x):
    hi = x.astype(jnp.bfloat16)
    rest = x - hi.astype(F32)
    mid = rest.astype(jnp.bfloat16)
    return hi, mid, (rest - mid.astype(F32)).astype(jnp.bfloat16)


def ldot(w, x):
    w = w.astype(jnp.bfloat16)
    hi, mid, lo = (jnp.dot(w, t, preferred_element_type=F32) for t in thirds(x))
    return hi + (mid + lo)


def rdot(x, w):
    w = w.astype(jnp.bfloat16)
    hi, mid, lo = (jnp.dot(t, w, preferred_element_type=F32) for t in thirds(x))
    return hi + (mid + lo)


def up1(v):
    return pltpu.roll(v, v.shape[0] - 1, 0)


def dn1(v):
    return pltpu.roll(v, 1, 0)


def lup(v):
    return pltpu.roll(v, v.shape[1] - 1, 1)


def ldn(v):
    return pltpu.roll(v, 1, 1)


def interp(out_cell, in_cell):
    home = out_cell >> 1
    near = jnp.where((out_cell & 1) == 0, home - 1, home + 1)
    return jnp.where(in_cell == home, 0.75, 0.0).astype(F32) + jnp.where(in_cell == near, 0.25, 0.0).astype(F32)


def pair_sum(fine, coarse):
    r, c = iota((fine, coarse), 0), iota((fine, coarse), 1)
    return jnp.where((r >> 1) == c, 1.0, 0.0).astype(F32)


class Level:
    def __init__(self, refs, planes, rows, lanes, zfull):
        self.c, self.wx, self.wy, self.wz, self.dg, self.iv = refs
        self.planes, self.rows, self.lanes, self.zfull = planes, rows, lanes, zfull

    def build(self, mask_of, lo, hi):
        lane = iota((self.rows, self.lanes), 1)
        c = self.c[lo - 1]
        for i in range(lo - 1, hi):
            nxt = self.c[i + 1]
            wxp = 0.5 * (c + nxt)
            self.wx[i] = wxp
            if i >= lo:
                wyp = 0.5 * (c + up1(c))
                wym = dn1(wyp)
                if self.zfull:
                    wzp = 0.5 * (c + jnp.where(lane == self.lanes - 1, 0.0, lup(c)))
                    wzm = 0.5 * (c + jnp.where(lane == 0, 0.0, ldn(c)))
                    wz = jnp.where(lane == self.lanes - 1, 0.0, wzp)
                else:
                    wzp = 0.5 * (c + lup(c))
                    wzm = ldn(wzp)
                    wz = wzp
                diag = wxp + self.wx[i - 1] + wyp + wym + wzp + wzm
                m = mask_of(i)
                self.wy[i] = wyp
                self.wz[i] = wz
                self.dg[i] = diag
                self.iv[i] = m / jnp.where(diag > 0.0, diag, 1.0)
            c = nxt

    def apply(self, v, i):
        x = v[i]
        s = self.wx[i] * v[i + 1] + self.wx[i - 1] * v[i - 1]
        wy = self.wy[i]
        s = s + wy * up1(x) + dn1(wy * x)
        wz = self.wz[i]
        s = s + wz * lup(x) + ldn(wz * x)
        return self.dg[i] * x - s


def body_kernel(f_hbm, c_hbm, o_ref,
                f_ref, c_ref, sy, sc, rxf, rxc, ry, rc, sux, suy, rux, ruy, ruc, f0, v0a, v0b, l0,
                sc1, rc1, sf1, rf1, su1, ru1, f1, u1, v1a, v1b, l1,
                sc2, gc2, ac2, rc2, sf2, gf2, af2, rf2, f2, v2a, v2b, d2, l2,
                r0b, r1b, lp1, lp0, rz0, rz1, pz1, pz0, hw, hx, y1, y0, yout,
                sg1, rg1, sg2, rg2, ssem, rsem, gsem, far):
    mx, my = lax.axis_index("gx"), lax.axis_index("gy")

    def dev(a, b):
        return (lax.rem(mx + (a + NXD), NXD), lax.rem(my + (b + NYD), NYD))

    partners = [(a, b) for a, b in NEAR if a and b]
    partners += [(0, b) for b in range(-R2, R2 + 1) if b] + [(a, 0) for a in range(-R2, R2 + 1) if a]
    barrier = pltpu.get_barrier_semaphore()
    for a, b in partners:
        pl.semaphore_signal(barrier, inc=1, device_id=dev(a, b), device_id_type=MESH)

    get_c = pltpu.make_async_copy(c_hbm, c_ref, gsem.at[4])
    get_f = pltpu.make_async_copy(f_hbm, f_ref, gsem.at[5])
    get_c.start()
    get_f.start()
    sends = []

    def send(src, dst, a, b):
        k = len(sends)
        copy = pltpu.make_async_remote_copy(src_ref=src, dst_ref=dst, send_sem=ssem.at[k], recv_sem=rsem.at[k],
                                            device_id=dev(a, b), device_id_type=MESH)
        copy.start()
        sends.append(copy)
        return copy

    def pack2(v):
        return v[0:2] + pltpu.roll(v[2:4], 64, 1)

    o, q = iota((4, 64), 0), iota((4, 64), 1)
    lc2 = jnp.where(((q >> 5) == (o >> 1)) & (((q & 7) >> 2) == (o & 1)), 0.015625, 0.0).astype(F32)
    o, q = iota((256, 128), 0), iota((256, 128), 1)
    zc2 = jnp.where((o >> 2) == q, 1.0, 0.0).astype(F32)
    get_c.wait()
    sc2[...] = pack2(rdot(ldot(lc2, c_ref[...].reshape(64, 256)), zc2))
    get_f.wait()
    for p in range(8):
        fp, cp = f_ref[p], c_ref[p]
        for s in (0, 1):
            sy[s, 0, p] = fp[4 * s : 4 * s + 4]
            sy[s, 1, p] = cp[4 * s : 4 * s + 4]
    for sx in (0, 1):
        for s in (0, 1):
            sc[sx, s, 0] = c_ref[6 * sx, 6 * s : 6 * s + 2]
            sc[sx, s, 1] = c_ref[6 * sx + 1, 6 * s : 6 * s + 2]
            sc[sx, s, 2] = f_ref[7 * sx, 6 * s : 6 * s + 2]
    pl.semaphore_wait(barrier, len(partners))

    offs = [4, -4, 3, -3, 2, -2, 1, -1]
    offx = [2, -2, 3, -3, 1, -1, 4, -4]
    wait_c2 = [send(sc2, gc2.at[R2 - k], 0, k) for k in offs]
    wait_a = []
    for sx, a in ((1, 1), (0, -1)):
        for s, b in ((1, 1), (0, -1)):
            wait_a.append(send(sc.at[sx, s], rc.at[1 - sx, 1 - s], a, b))
    for s, a in ((1, 1), (0, -1)):
        wait_a.append(send(c_ref.at[5:8] if s else c_ref.at[0:3], rxc.at[1 - s], a, 0))
        wait_a.append(send(f_ref.at[6:8] if s else f_ref.at[0:2], rxf.at[1 - s], a, 0))
    for s, b in ((1, 1), (0, -1)):
        wait_a.append(send(sy.at[s], ry.at[1 - s], 0, b))
    rz0[...] = pair_sum(256, 128)
    rz1[...] = pair_sum(128, 128)
    o, q = iota((16, 64), 0), iota((16, 64), 1)
    lc1 = jnp.where(((q >> 4) == (o >> 2)) & (((q & 7) >> 1) == (o & 3)), 0.125, 0.0).astype(F32)
    sc1[...] = rdot(ldot(lc1, c_ref[...].reshape(64, 256)), rz0[...]).reshape(4, 4, 128)
    wait_c1 = [send(sc1, rc1.at[n], a, b) for n, (a, b) in enumerate(NEAR)]

    zed = jnp.zeros((16, 256), F32)
    for p in (0, 1, 2, 3, 12, 13, 14, 15):
        f0[p] = zed
        l0[0][p] = zed

    o, q = iota((16, 128), 0), iota((16, 128), 1)
    yr = (q & 15) - 4
    lr0 = jnp.where(((q >> 5) == (o >> 2)) & ((yr >> 1) == (o & 3)) & (yr >= 0) & (yr < 8), 0.5, 0.0).astype(F32)
    o, q = iota((4, 64), 0), iota((4, 64), 1)
    yr = (q & 15) - 4
    lr1 = jnp.where(((q >> 5) == (o >> 1)) & ((yr >> 1) == (o & 1)) & (yr >= 0) & (yr < 4), 0.5, 0.0).astype(F32)

    def prolong_matrix(planes_out, x_out0, x_in0, rows_in, planes_in, y_out0, y_in0, bx, by, nx, ny):
        shape = (planes_out * 16, planes_in * rows_in)
        r, c = iota(shape, 0), iota(shape, 1)
        xo, yo = (r >> 4) + x_out0, (r & 15) + y_out0
        if rows_in == 16:
            ci, cr = c >> 4, c & 15
        else:
            ci = (c * 2731) >> 16
            cr = c - ci * rows_in
        w = interp(xo, ci + x_in0) * interp(yo, cr + y_in0)
        gx_, gy_ = xo + mx * bx, yo + my * by
        ok = (gx_ >= 0) & (gx_ < nx) & (gy_ >= 0) & (gy_ < ny)
        return jnp.where(ok, w, 0.0)

    lp1[...] = prolong_matrix(12, -4, -3, 24, 8, -4, -H2, 4, 4, 64, 128)
    lp0[...] = prolong_matrix(12, -2, -2, 16, 8, -4, -4, 8, 8, 128, 256)
    r, c = iota((128, 128), 0), iota((128, 128), 1)
    pz1[...] = jnp.where(r < 64, interp(c, r), 0.0)
    r, c = iota((128, 256), 0), iota((128, 256), 1)
    pz0[...] = interp(c, r)

    def masker(rows, lanes, halo, b, nx, ny, valid_lanes, valid_rows):
        row = iota((rows, lanes), 0)
        y = row - halo + my * b
        ok = (y >= 0) & (y < ny) & (row < valid_rows)
        if valid_lanes < lanes:
            ok = ok & (iota((rows, lanes), 1) < valid_lanes)
        base = jnp.where(ok, 1.0, 0.0).astype(F32)

        def mask_of(i):
            x = mx * b + (i - halo)
            return base * jnp.where((x >= 0) & (x < nx), 1.0, 0.0).astype(F32)

        return mask_of

    mask0 = masker(16, 256, 4, 8, NX, NY, 256, 16)
    mask1 = masker(16, 128, 4, 4, NX // 2, NY // 2, 128, 12)
    mask2 = masker(24, 128, H2, 2, NX // 4, NY // 4, 64, 2 * H2 + 2)

    def gather2(mine, got, rows):
        rows[...] = jnp.zeros((24, 128), F32)
        rows[H2 : H2 + 2] = mine[...]
        for k in offs:
            rows[2 * (k + R2) : 2 * (k + R2) + 2] = got[k + R2]

    def unpack2(mine, got, cells):
        for k in [0] + offs:
            v = mine[...] if k == 0 else got[k + R2]
            i = 2 * (k + R2)
            cells[i] = v * mask2(i)
            cells[i + 1] = pltpu.roll(v, 64, 1) * mask2(i + 1)

    def spread1(mine, got, cells):
        for n, (a, b) in enumerate([(0, 0)] + NEAR):
            for p in range(4):
                x, y = 4 - 4 * a + p, 4 - 4 * b
                cells[x, y : y + 4] = mine[p] if n == 0 else got[n - 1, p]

    for w in wait_c2:
        w.wait_recv()
    for b in (8, -8):
        pl.semaphore_signal(far, inc=1, device_id=dev(0, b), device_id_type=MESH)
    gather2(sc2, gc2, ac2)
    wait_c2 = [send(ac2, rc2.at[R2 - k], k, 0) for k in offx]

    zed1 = jnp.zeros((4, 128), F32)
    for i in range(12):
        l1[0][i, 12:16] = zed1
        f1[i, 12:16] = zed1
        u1[i, 12:16] = zed1
    for w in wait_c1:
        w.wait_recv()
    spread1(sc1, rc1, l1[0])
    for i in range(12):
        l1[0][i] = l1[0][i] * mask1(i)
    lev1 = Level(l1, 12, 16, 128, True)
    lev1.build(mask1, 1, 11)

    for w in wait_a:
        w.wait_recv()
    c0 = l0[0]
    for p in range(8):
        i = p + 4
        f0[i, 0:4] = ry[0, 0, p]
        f0[i, 4:12] = f_ref[p]
        f0[i, 12:16] = ry[1, 0, p]
        c0[i, 0:4] = ry[0, 1, p]
        c0[i, 4:12] = c_ref[p]
        c0[i, 12:16] = ry[1, 1, p]
    for p in range(3):
        c0[1 + p, 4:12] = rxc[0, p]
        c0[12 + p, 4:12] = rxc[1, p]
    for p in range(2):
        f0[2 + p, 4:12] = rxf[0, p]
        f0[12 + p, 4:12] = rxf[1, p]
        for s in (0, 1):
            c0[2 + p, 2 + 10 * s : 4 + 10 * s] = rc[0, s, p]
            c0[12 + p, 2 + 10 * s : 4 + 10 * s] = rc[1, s, p]
    for s in (0, 1):
        f0[3, 2 + 10 * s : 4 + 10 * s] = rc[0, s, 2]
        f0[12, 2 + 10 * s : 4 + 10 * s] = rc[1, s, 2]
    for i in range(16):
        c0[i] = c0[i] * mask0(i)
    lev0 = Level(l0, 16, 16, 256, True)
    lev0.build(mask0, 2, 14)

    inv_mid, ((keep, push),) = chebyshev(SMOOTH_LOW, SMOOTH_HIGH, 2)

    def first(lev, f, v, lo, hi):
        for i in range(lo, hi):
            v[i] = f[i] * lev.iv[i] * inv_mid

    def second(lev, f, va, vb, lo, hi):
        for i in range(lo, hi):
            d = va[i]
            r = f[i] - lev.apply(va, i)
            vb[i] = d + (keep * d + push * (r * lev.iv[i]))

    def residual(lev, f, v, out, lo, hi):
        for i in range(lo, hi):
            out[i - lo] = f[i] - lev.apply(v, i)

    first(lev0, f0, v0a, 2, 14)
    second(lev0, f0, v0a, v0b, 3, 13)
    residual(lev0, f0, v0b, r0b, 4, 12)
    f1own = rdot(ldot(lr0, r0b[...].reshape(128, 256)), rz0[...])
    sf1[...] = f1own.reshape(4, 4, 128)
    wait_f1 = [send(sf1, rf1.at[n], a, b) for n, (a, b) in enumerate(NEAR)]

    for p in range(8):
        for s in (0, 1):
            suy[s, p] = v0b[4 + p, 4 + 6 * s : 6 + 6 * s]
    for p in range(2):
        for s in (0, 1):
            sux[s, p] = v0b[4 + 6 * s + p, 4:12]
    wait_u0 = []
    for sx, a in ((1, 1), (0, -1)):
        for s, b in ((1, 1), (0, -1)):
            wait_u0.append(send(suy.at[s, 7 * sx], ruc.at[1 - sx, 1 - s], a, b))
    wait_u0 += [send(sux.at[s], rux.at[1 - s], a, 0) for s, a in ((1, 1), (0, -1))]
    wait_u0 += [send(suy.at[s], ruy.at[1 - s], 0, b) for s, b in ((1, 1), (0, -1))]

    for w in wait_c2:
        w.wait_recv()
    unpack2(ac2, rc2, l2[0])
    lev2 = Level(l2, 18, 24, 128, False)
    lev2.build(mask2, 1, 17)

    def rhs(lev, f, v, i):
        return -lev.apply(v, i) if f is None else f[i] - lev.apply(v, i)

    def post(lev, f, v, w, lo, hi, out=None):
        for i in range(lo, hi):
            w[i] = v[i] + rhs(lev, f, v, i) * lev.iv[i] * inv_mid
        for i in range(lo + 1, hi - 1):
            d = w[i] - v[i]
            e = w[i] + (keep * d + push * (rhs(lev, f, w, i) * lev.iv[i]))
            if out is None:
                v[i] = e
            else:
                out[i - lo - 1] = e[4:12]

    mid2, pairs2 = chebyshev(COARSE_LOW, COARSE_HIGH, COARSE_STEPS)
    row = iota((24, 128), 0)
    own = jnp.where((row == H2) | (row == H2 + 1), 1.0, 0.0).astype(F32)
    for i in range(1, 17):
        v2a[i] = mask2(i)
    den = jnp.zeros((24, 128), F32)
    va, vb = v2a, v2b
    for m, (k2, p2) in enumerate([(0.0, mid2)] + pairs2):
        for i in range(2 + m, 16 - m):
            r = lev2.apply(va, i)
            if m == 0 and i in (H2, H2 + 1):
                den = den + own * mask2(i) * r
            d = -p2 * (r * lev2.iv[i])
            if m:
                d = k2 * d2[i] + d
            d2[i] = d
            vb[i] = va[i] + d
        va, vb = vb, va
    r, c = iota((128, 96), 0), iota((128, 96), 1)
    ci = (c * 2731) >> 16
    spread = ((((r >> 4) - 2) >> 1) == ci - 1) & ((((r & 15) - 4) >> 1) == c - ci * 24 - H2)
    spread = jnp.where(spread, 0.5, 0.0).astype(F32)
    r, c = iota((128, 128), 0), iota((128, 128), 1)
    hw[2:10] = rdot(ldot(spread, va[7:11].reshape(96, 128)), jnp.where((c >> 1) == r, 1.0, 0.0).astype(F32)).reshape(8, 16, 128)
    post(lev1, None, hw, hx, 3, 9)
    num = jnp.zeros((4, 128), F32)
    for p in range(4):
        num = num + hw[4 + p, 4:8] * sf1[p]
    sg1[0:1] = jnp.sum(num, axis=0, keepdims=True)
    sg1[1:2] = jnp.sum(den, axis=0, keepdims=True)

    def broadcast(mine, got, count, offset_of, k):
        for n in sorted(range(1, count), key=lambda n: abs(n - count // 2)):
            copy = pltpu.make_async_remote_copy(src_ref=mine, dst_ref=got.at[n - 1], send_sem=gsem.at[2 * k], recv_sem=gsem.at[2 * k + 1],
                                                device_id=dev(*offset_of(n)), device_id_type=MESH)
            copy.start()
        return pltpu.make_async_remote_copy(src_ref=got, dst_ref=got, send_sem=gsem.at[2 * k], recv_sem=gsem.at[2 * k + 1],
                                            device_id=dev(*offset_of(1)), device_id_type=MESH)

    pl.semaphore_wait(far, 2)
    all_y = broadcast(sg1, rg1, NYD, lambda n: (0, n), 0)

    for w in wait_f1:
        w.wait_recv()
    spread1(sf1, rf1, f1)
    first(lev1, f1, v1a, 1, 11)
    second(lev1, f1, v1a, v1b, 2, 10)
    residual(lev1, f1, v1b, r1b, 4, 8)
    f2own = rdot(ldot(lr1, r1b[...].reshape(64, 128)), rz1[...])
    g0 = f2own[0:2] * lev2.iv[H2, H2 : H2 + 2] * mid2
    g1 = f2own[2:4] * lev2.iv[H2 + 1, H2 : H2 + 2] * mid2
    sf2[...] = g0 + pltpu.roll(g1, 64, 1)
    wait_f2 = [send(sf2, gf2.at[R2 - k], 0, k) for k in offs]
    for p in range(4):
        su1[p] = v1b[4 + p, 4:8]
    wait_u1 = [send(su1, ru1.at[n], a, b) for n, (a, b) in enumerate(NEAR)]

    ones = jnp.concatenate([mask2(i) for i in range(5, 13)], axis=0)
    y1[...] = rdot(ldot(lp1[...], ones), pz1[...]).reshape(12, 16, 128)
    post(lev1, None, y1, v1a, 1, 11)
    y0[2:14] = rdot(ldot(lp0[...], y1[2:10].reshape(128, 128)), pz0[...]).reshape(12, 16, 256)
    post(lev0, None, y0, v0a, 3, 13, yout)

    for w in wait_f2:
        w.wait_recv()
    gather2(sf2, gf2, af2)
    wait_f2 = [send(af2, rf2.at[R2 - k], k, 0) for k in offx]

    for w in wait_u1:
        w.wait_recv()
    spread1(su1, ru1, u1)
    for i in range(12):
        u1[i] = u1[i] * mask1(i)

    for w in wait_u0:
        w.wait_recv()
    for p in range(8):
        v0b[4 + p, 2:4] = ruy[0, p]
        v0b[4 + p, 12:14] = ruy[1, p]
    for i in (2, 3, 12, 13):
        v0b[i] = zed
    for p in range(2):
        v0b[2 + p, 4:12] = rux[0, p]
        v0b[12 + p, 4:12] = rux[1, p]
    for s in (0, 1):
        v0b[3, 2 + 10 * s : 4 + 10 * s] = ruc[0, s]
        v0b[12, 2 + 10 * s : 4 + 10 * s] = ruc[1, s]
    for i in range(2, 14):
        v0b[i] = v0b[i] * mask0(i)

    all_y.wait_recv()
    sg2[...] = sg1[...] + jnp.sum(rg1[...], axis=0)
    all_x = broadcast(sg2, rg2, NXD, lambda n: (n, 0), 1)

    for w in wait_f2:
        w.wait_recv()
    unpack2(af2, rf2, v2a)
    for i in range(1, 17):
        d = v2a[i]
        d2[i] = d
        f2[i] = d * (lev2.dg[i] * (1.0 / mid2))
    va, vb = v2a, v2b
    for m, (k2, p2) in enumerate(pairs2):
        for i in range(1 + m, 17 - m):
            r = f2[i] - lev2.apply(va, i)
            d = k2 * d2[i] + p2 * (r * lev2.iv[i])
            d2[i] = d
            vb[i] = va[i] + d
        va, vb = vb, va

    p1 = rdot(ldot(lp1[...], va[5:13].reshape(192, 128)), pz1[...]).reshape(12, 16, 128)
    for i in range(12):
        u1[i] = u1[i] + p1[i]
    post(lev1, f1, u1, v1a, 1, 11)
    p0 = rdot(ldot(lp0[...], u1[2:10].reshape(128, 128)), pz0[...]).reshape(12, 16, 256)
    for i in range(12):
        v0b[i + 2] = v0b[i + 2] + p0[i]
    post(lev0, f0, v0b, v0a, 3, 13, o_ref)

    all_x.wait_recv()
    total = sg2[...] + jnp.sum(rg2[...], axis=0)
    shift = jnp.sum(total[0:1], axis=1, keepdims=True) / jnp.sum(total[1:2], axis=1, keepdims=True)
    for p in range(8):
        o_ref[p] = o_ref[p] + shift * yout[p]
    all_y.wait_send()
    all_x.wait_send()

    for w in sends:
        w.wait_send()


def solution(mesh):
    def vm(*shape):
        return pltpu.VMEM(shape, F32)

    def level(*shape):
        return [vm(*shape) for _ in range(6)]

    nsend = 4 + 4 + 2 + 8 + 8 + 8 + 8 + 8 + 8 + 8 + 8
    scratch = [
        vm(8, 8, 256), vm(8, 8, 256), vm(2, 2, 8, 4, 256), vm(2, 2, 3, 2, 256), vm(2, 2, 8, 256), vm(2, 3, 8, 256), vm(2, 2, 8, 4, 256),
        vm(2, 2, 3, 2, 256), vm(2, 2, 8, 256), vm(2, 8, 2, 256), vm(2, 2, 8, 256), vm(2, 8, 2, 256), vm(2, 2, 2, 256),
        vm(16, 16, 256), vm(16, 16, 256), vm(16, 16, 256), level(16, 16, 256),
        vm(4, 4, 128), vm(8, 4, 4, 128), vm(4, 4, 128), vm(8, 4, 4, 128), vm(4, 4, 128), vm(8, 4, 4, 128),
        vm(12, 16, 128), vm(12, 16, 128), vm(12, 16, 128), vm(12, 16, 128), level(12, 16, 128),
        vm(2, 128), vm(9, 2, 128), vm(24, 128), vm(9, 24, 128), vm(2, 128), vm(9, 2, 128), vm(24, 128), vm(9, 24, 128),
        vm(18, 24, 128), vm(18, 24, 128), vm(18, 24, 128), vm(18, 24, 128), level(18, 24, 128),
        vm(8, 16, 256), vm(4, 16, 128), vm(192, 192), vm(192, 128), vm(256, 128), vm(128, 128), vm(128, 128), vm(128, 256),
        vm(12, 16, 128), vm(12, 16, 128), vm(12, 16, 128), vm(16, 16, 256), vm(8, 8, 256),
        vm(2, 128), vm(NYD - 1, 2, 128), vm(2, 128), vm(NXD - 1, 2, 128),
        pltpu.SemaphoreType.DMA((nsend,)), pltpu.SemaphoreType.DMA((nsend,)), pltpu.SemaphoreType.DMA((6,)), pltpu.SemaphoreType.REGULAR,
    ]

    def body(right_side, coefficient):
        return pl.pallas_call(
            body_kernel,
            out_shape=jax.ShapeDtypeStruct((8, 8, 256), F32),
            in_specs=[pl.BlockSpec(memory_space=pl.ANY)] * 2,
            out_specs=pl.BlockSpec(memory_space=pltpu.VMEM),
            scratch_shapes=scratch,
            compiler_params=pltpu.CompilerParams(collective_id=0, has_side_effects=True),
        )(right_side, coefficient)

    placed = (P("gx", "gy", None), P("gx", "gy", None))
    return jax.shard_map(body, mesh=mesh, in_specs=placed, out_specs=P("gx", "gy", None), check_vma=False)
```

```python
import jax
import jax.numpy as jnp
from jax import lax
from jax.experimental import pallas as pl
from jax.experimental.pallas import tpu as pltpu
from jax.sharding import PartitionSpec as P

SMOOTH_LOW = 0.5
SMOOTH_HIGH = 2.0
COARSE_LOW = 0.05
COARSE_HIGH = 2.0
COARSE_STEPS = 6

F32 = jnp.float32
NXD, NYD = 16, 32
NX, NY, NZ = 128, 256, 256
R2 = 4
H2 = 2 * R2
MESH = pl.DeviceIdType.MESH
NEAR = [(1, 1), (1, -1), (-1, 1), (-1, -1), (1, 0), (-1, 0), (0, 1), (0, -1)]


def chebyshev(low_end, high_end, sweeps):
    middle = 0.5 * (high_end + low_end)
    half_span = 0.5 * (high_end - low_end)
    sig_ratio = middle / half_span
    rho_now = 1.0 / sig_ratio
    pairs = []
    for _ in range(1, sweeps):
        rho_next = 1.0 / (2.0 * sig_ratio - rho_now)
        pairs.append((rho_next * rho_now, 2.0 * rho_next / half_span))
        rho_now = rho_next
    return 1.0 / middle, pairs


def iota(shape, dim):
    return lax.broadcasted_iota(jnp.int32, shape, dim)


def thirds(x):
    hi = x.astype(jnp.bfloat16)
    rest = x - hi.astype(F32)
    mid = rest.astype(jnp.bfloat16)
    return hi, mid, (rest - mid.astype(F32)).astype(jnp.bfloat16)


def ldot(w, x):
    w = w.astype(jnp.bfloat16)
    hi, mid, lo = (jnp.dot(w, t, preferred_element_type=F32) for t in thirds(x))
    return hi + (mid + lo)


def rdot(x, w):
    w = w.astype(jnp.bfloat16)
    hi, mid, lo = (jnp.dot(t, w, preferred_element_type=F32) for t in thirds(x))
    return hi + (mid + lo)


def up1(v):
    return pltpu.roll(v, v.shape[0] - 1, 0)


def dn1(v):
    return pltpu.roll(v, 1, 0)


def lup(v):
    return pltpu.roll(v, v.shape[1] - 1, 1)


def ldn(v):
    return pltpu.roll(v, 1, 1)


def interp(out_cell, in_cell):
    home = out_cell >> 1
    near = jnp.where((out_cell & 1) == 0, home - 1, home + 1)
    return jnp.where(in_cell == home, 0.75, 0.0).astype(F32) + jnp.where(in_cell == near, 0.25, 0.0).astype(F32)


def pair_sum(fine, coarse):
    r, c = iota((fine, coarse), 0), iota((fine, coarse), 1)
    return jnp.where((r >> 1) == c, 1.0, 0.0).astype(F32)


class Level:
    def __init__(self, refs, planes, rows, lanes, zfull):
        self.c, self.wx, self.wy, self.wz, self.dg, self.iv = refs
        self.planes, self.rows, self.lanes, self.zfull = planes, rows, lanes, zfull

    def build(self, mask_of, lo, hi):
        lane = iota((self.rows, self.lanes), 1)
        c = self.c[lo - 1]
        for i in range(lo - 1, hi):
            nxt = self.c[i + 1]
            wxp = 0.5 * (c + nxt)
            self.wx[i] = wxp
            if i >= lo:
                wyp = 0.5 * (c + up1(c))
                wym = dn1(wyp)
                if self.zfull:
                    wzp = 0.5 * (c + jnp.where(lane == self.lanes - 1, 0.0, lup(c)))
                    wzm = 0.5 * (c + jnp.where(lane == 0, 0.0, ldn(c)))
                    wz = jnp.where(lane == self.lanes - 1, 0.0, wzp)
                else:
                    wzp = 0.5 * (c + lup(c))
                    wzm = ldn(wzp)
                    wz = wzp
                diag = wxp + self.wx[i - 1] + wyp + wym + wzp + wzm
                m = mask_of(i)
                self.wy[i] = wyp
                self.wz[i] = wz
                self.dg[i] = diag
                self.iv[i] = m / jnp.where(diag > 0.0, diag, 1.0)
            c = nxt

    def apply(self, v, i):
        x = v[i]
        s = self.wx[i] * v[i + 1] + self.wx[i - 1] * v[i - 1]
        wy = self.wy[i]
        s = s + wy * up1(x) + dn1(wy * x)
        wz = self.wz[i]
        s = s + wz * lup(x) + ldn(wz * x)
        return self.dg[i] * x - s


def body_kernel(f_hbm, c_hbm, o_ref,
                f_ref, c_ref, sy, sc, rxf, rxc, ry, rc, sux, suy, rux, ruy, ruc, f0, v0a, v0b, l0,
                sc1, rc1, sf1, rf1, su1, ru1, f1, u1, v1a, v1b, l1,
                sc2, gc2, ac2, rc2, sf2, gf2, af2, rf2, f2, v2a, v2b, d2, l2,
                r0b, r1b, lp1, lp0, rz0, rz1, pz1, pz0, hw, hx, y1, y0, yout,
                sg1, rg1, sg2, rg2, ssem, rsem, gsem, far):
    mx, my = lax.axis_index("gx"), lax.axis_index("gy")

    def dev(a, b):
        return (lax.rem(mx + (a + NXD), NXD), lax.rem(my + (b + NYD), NYD))

    get_c = pltpu.make_async_copy(c_hbm, c_ref, gsem.at[4])
    get_f = pltpu.make_async_copy(f_hbm, f_ref, gsem.at[5])
    get_c.start()
    get_f.start()
    partners = [(a, b) for a, b in NEAR if a and b]
    partners += [(0, b) for b in range(-R2, R2 + 1) if b] + [(a, 0) for a in range(-R2, R2 + 1) if a]
    barrier = pltpu.get_barrier_semaphore()
    for a, b in partners:
        pl.semaphore_signal(barrier, inc=1, device_id=dev(a, b), device_id_type=MESH)

    sends = []

    def send(src, dst, a, b):
        k = len(sends)
        copy = pltpu.make_async_remote_copy(src_ref=src, dst_ref=dst, send_sem=ssem.at[k], recv_sem=rsem.at[k],
                                            device_id=dev(a, b), device_id_type=MESH)
        copy.start()
        sends.append(copy)
        return copy

    def pack2(v):
        return v[0:2] + pltpu.roll(v[2:4], 64, 1)

    o, q = iota((4, 64), 0), iota((4, 64), 1)
    lc2 = jnp.where(((q >> 5) == (o >> 1)) & (((q & 7) >> 2) == (o & 1)), 0.015625, 0.0).astype(F32)
    o, q = iota((256, 128), 0), iota((256, 128), 1)
    zc2 = jnp.where((o >> 2) == q, 1.0, 0.0).astype(F32)
    get_c.wait()
    sc2[...] = pack2(rdot(ldot(lc2, c_ref[...].reshape(64, 256)), zc2))
    get_f.wait()
    for p in range(8):
        fp, cp = f_ref[p], c_ref[p]
        for s in (0, 1):
            sy[s, 0, p] = fp[4 * s : 4 * s + 4]
            sy[s, 1, p] = cp[4 * s : 4 * s + 4]
    for sx in (0, 1):
        for s in (0, 1):
            sc[sx, s, 0] = c_ref[6 * sx, 6 * s : 6 * s + 2]
            sc[sx, s, 1] = c_ref[6 * sx + 1, 6 * s : 6 * s + 2]
            sc[sx, s, 2] = f_ref[7 * sx, 6 * s : 6 * s + 2]
    pl.semaphore_wait(barrier, len(partners))

    offs = [4, -4, 3, -3, 2, -2, 1, -1]
    offx = [2, -2, 3, -3, 1, -1, 4, -4]
    wait_c2 = [send(sc2, gc2.at[R2 - k], 0, k) for k in offs]
    wait_a = []
    for sx, a in ((1, 1), (0, -1)):
        for s, b in ((1, 1), (0, -1)):
            wait_a.append(send(sc.at[sx, s], rc.at[1 - sx, 1 - s], a, b))
    for s, a in ((1, 1), (0, -1)):
        wait_a.append(send(c_ref.at[5:8] if s else c_ref.at[0:3], rxc.at[1 - s], a, 0))
        wait_a.append(send(f_ref.at[6:8] if s else f_ref.at[0:2], rxf.at[1 - s], a, 0))
    for s, b in ((1, 1), (0, -1)):
        wait_a.append(send(sy.at[s], ry.at[1 - s], 0, b))
    rz0[...] = pair_sum(256, 128)
    rz1[...] = pair_sum(128, 128)
    o, q = iota((16, 64), 0), iota((16, 64), 1)
    lc1 = jnp.where(((q >> 4) == (o >> 2)) & (((q & 7) >> 1) == (o & 3)), 0.125, 0.0).astype(F32)
    sc1[...] = rdot(ldot(lc1, c_ref[...].reshape(64, 256)), rz0[...]).reshape(4, 4, 128)
    wait_c1 = [send(sc1, rc1.at[n], a, b) for n, (a, b) in enumerate(NEAR)]

    zed = jnp.zeros((16, 256), F32)
    for p in (0, 1, 2, 3, 12, 13, 14, 15):
        f0[p] = zed
        l0[0][p] = zed

    o, q = iota((16, 128), 0), iota((16, 128), 1)
    yr = (q & 15) - 4
    lr0 = jnp.where(((q >> 5) == (o >> 2)) & ((yr >> 1) == (o & 3)) & (yr >= 0) & (yr < 8), 0.5, 0.0).astype(F32)
    o, q = iota((4, 64), 0), iota((4, 64), 1)
    yr = (q & 15) - 4
    lr1 = jnp.where(((q >> 5) == (o >> 1)) & ((yr >> 1) == (o & 1)) & (yr >= 0) & (yr < 4), 0.5, 0.0).astype(F32)

    def prolong_matrix(planes_out, x_out0, x_in0, rows_in, planes_in, y_out0, y_in0, bx, by, nx, ny):
        shape = (planes_out * 16, planes_in * rows_in)
        r, c = iota(shape, 0), iota(shape, 1)
        xo, yo = (r >> 4) + x_out0, (r & 15) + y_out0
        if rows_in == 16:
            ci, cr = c >> 4, c & 15
        else:
            ci = (c * 2731) >> 16
            cr = c - ci * rows_in
        w = interp(xo, ci + x_in0) * interp(yo, cr + y_in0)
        gx_, gy_ = xo + mx * bx, yo + my * by
        ok = (gx_ >= 0) & (gx_ < nx) & (gy_ >= 0) & (gy_ < ny)
        return jnp.where(ok, w, 0.0)

    lp1[...] = prolong_matrix(12, -4, -3, 24, 8, -4, -H2, 4, 4, 64, 128)
    lp0[...] = prolong_matrix(12, -2, -2, 16, 8, -4, -4, 8, 8, 128, 256)
    r, c = iota((128, 128), 0), iota((128, 128), 1)
    pz1[...] = jnp.where(r < 64, interp(c, r), 0.0)
    r, c = iota((128, 256), 0), iota((128, 256), 1)
    pz0[...] = interp(c, r)

    def masker(rows, lanes, halo, b, nx, ny, valid_lanes, valid_rows):
        row = iota((rows, lanes), 0)
        y = row - halo + my * b
        ok = (y >= 0) & (y < ny) & (row < valid_rows)
        if valid_lanes < lanes:
            ok = ok & (iota((rows, lanes), 1) < valid_lanes)
        base = jnp.where(ok, 1.0, 0.0).astype(F32)

        def mask_of(i):
            x = mx * b + (i - halo)
            return base * jnp.where((x >= 0) & (x < nx), 1.0, 0.0).astype(F32)

        return mask_of

    mask0 = masker(16, 256, 4, 8, NX, NY, 256, 16)
    mask1 = masker(16, 128, 4, 4, NX // 2, NY // 2, 128, 12)
    mask2 = masker(24, 128, H2, 2, NX // 4, NY // 4, 64, 2 * H2 + 2)

    def gather2(mine, got, rows):
        rows[...] = jnp.zeros((24, 128), F32)
        rows[H2 : H2 + 2] = mine[...]
        for k in offs:
            rows[2 * (k + R2) : 2 * (k + R2) + 2] = got[k + R2]

    def unpack2(mine, got, cells):
        for k in [0] + offs:
            v = mine[...] if k == 0 else got[k + R2]
            i = 2 * (k + R2)
            cells[i] = v * mask2(i)
            cells[i + 1] = pltpu.roll(v, 64, 1) * mask2(i + 1)

    def spread1(mine, got, cells):
        for n, (a, b) in enumerate([(0, 0)] + NEAR):
            for p in range(4):
                x, y = 4 - 4 * a + p, 4 - 4 * b
                cells[x, y : y + 4] = mine[p] if n == 0 else got[n - 1, p]

    for w in wait_c2:
        w.wait_recv()
    for b in (8, -8):
        pl.semaphore_signal(far, inc=1, device_id=dev(0, b), device_id_type=MESH)
    gather2(sc2, gc2, ac2)
    wait_c2 = [send(ac2, rc2.at[R2 - k], k, 0) for k in offx]

    zed1 = jnp.zeros((4, 128), F32)
    for i in range(12):
        l1[0][i, 12:16] = zed1
        f1[i, 12:16] = zed1
        u1[i, 12:16] = zed1
    for w in wait_c1:
        w.wait_recv()
    spread1(sc1, rc1, l1[0])
    for i in range(12):
        l1[0][i] = l1[0][i] * mask1(i)
    lev1 = Level(l1, 12, 16, 128, True)
    lev1.build(mask1, 1, 11)

    for w in wait_a:
        w.wait_recv()
    c0 = l0[0]
    for p in range(8):
        i = p + 4
        f0[i, 0:4] = ry[0, 0, p]
        f0[i, 4:12] = f_ref[p]
        f0[i, 12:16] = ry[1, 0, p]
        c0[i, 0:4] = ry[0, 1, p]
        c0[i, 4:12] = c_ref[p]
        c0[i, 12:16] = ry[1, 1, p]
    for p in range(3):
        c0[1 + p, 4:12] = rxc[0, p]
        c0[12 + p, 4:12] = rxc[1, p]
    for p in range(2):
        f0[2 + p, 4:12] = rxf[0, p]
        f0[12 + p, 4:12] = rxf[1, p]
        for s in (0, 1):
            c0[2 + p, 2 + 10 * s : 4 + 10 * s] = rc[0, s, p]
            c0[12 + p, 2 + 10 * s : 4 + 10 * s] = rc[1, s, p]
    for s in (0, 1):
        f0[3, 2 + 10 * s : 4 + 10 * s] = rc[0, s, 2]
        f0[12, 2 + 10 * s : 4 + 10 * s] = rc[1, s, 2]
    for i in range(16):
        c0[i] = c0[i] * mask0(i)
    lev0 = Level(l0, 16, 16, 256, True)
    lev0.build(mask0, 2, 14)

    inv_mid, ((keep, push),) = chebyshev(SMOOTH_LOW, SMOOTH_HIGH, 2)

    def first(lev, f, v, lo, hi):
        for i in range(lo, hi):
            v[i] = f[i] * lev.iv[i] * inv_mid

    def second(lev, f, va, vb, lo, hi):
        for i in range(lo, hi):
            d = va[i]
            r = f[i] - lev.apply(va, i)
            vb[i] = d + (keep * d + push * (r * lev.iv[i]))

    def residual(lev, f, v, out, lo, hi):
        for i in range(lo, hi):
            out[i - lo] = f[i] - lev.apply(v, i)

    first(lev0, f0, v0a, 2, 14)
    second(lev0, f0, v0a, v0b, 3, 13)
    residual(lev0, f0, v0b, r0b, 4, 12)
    f1own = rdot(ldot(lr0, r0b[...].reshape(128, 256)), rz0[...])
    sf1[...] = f1own.reshape(4, 4, 128)
    wait_f1 = [send(sf1, rf1.at[n], a, b) for n, (a, b) in enumerate(NEAR)]

    for p in range(8):
        for s in (0, 1):
            suy[s, p] = v0b[4 + p, 4 + 6 * s : 6 + 6 * s]
    for p in range(2):
        for s in (0, 1):
            sux[s, p] = v0b[4 + 6 * s + p, 4:12]
    wait_u0 = []
    for sx, a in ((1, 1), (0, -1)):
        for s, b in ((1, 1), (0, -1)):
            wait_u0.append(send(suy.at[s, 7 * sx], ruc.at[1 - sx, 1 - s], a, b))
    wait_u0 += [send(sux.at[s], rux.at[1 - s], a, 0) for s, a in ((1, 1), (0, -1))]
    wait_u0 += [send(suy.at[s], ruy.at[1 - s], 0, b) for s, b in ((1, 1), (0, -1))]

    for w in wait_c2:
        w.wait_recv()
    unpack2(ac2, rc2, l2[0])
    lev2 = Level(l2, 18, 24, 128, False)
    lev2.build(mask2, 1, 17)

    def rhs(lev, f, v, i):
        return -lev.apply(v, i) if f is None else f[i] - lev.apply(v, i)

    def post(lev, f, v, w, lo, hi, out=None):
        for i in range(lo, hi):
            w[i] = v[i] + rhs(lev, f, v, i) * lev.iv[i] * inv_mid
        for i in range(lo + 1, hi - 1):
            d = w[i] - v[i]
            e = w[i] + (keep * d + push * (rhs(lev, f, w, i) * lev.iv[i]))
            if out is None:
                v[i] = e
            else:
                out[i - lo - 1] = e[4:12]

    mid2, pairs2 = chebyshev(COARSE_LOW, COARSE_HIGH, COARSE_STEPS)
    row = iota((24, 128), 0)
    own = jnp.where((row == H2) | (row == H2 + 1), 1.0, 0.0).astype(F32)
    for i in range(1, 17):
        v2a[i] = mask2(i)
    den = jnp.zeros((24, 128), F32)
    va, vb = v2a, v2b
    for m, (k2, p2) in enumerate([(0.0, mid2)] + pairs2):
        for i in range(2 + m, 16 - m):
            r = lev2.apply(va, i)
            if m == 0 and i in (H2, H2 + 1):
                den = den + own * mask2(i) * r
            d = -p2 * (r * lev2.iv[i])
            if m:
                d = k2 * d2[i] + d
            d2[i] = d
            vb[i] = va[i] + d
        va, vb = vb, va
    r, c = iota((128, 96), 0), iota((128, 96), 1)
    ci = (c * 2731) >> 16
    spread = ((((r >> 4) - 2) >> 1) == ci - 1) & ((((r & 15) - 4) >> 1) == c - ci * 24 - H2)
    spread = jnp.where(spread, 0.5, 0.0).astype(F32)
    r, c = iota((128, 128), 0), iota((128, 128), 1)
    hw[2:10] = rdot(ldot(spread, va[7:11].reshape(96, 128)), jnp.where((c >> 1) == r, 1.0, 0.0).astype(F32)).reshape(8, 16, 128)
    post(lev1, None, hw, hx, 3, 9)
    num = jnp.zeros((4, 128), F32)
    for p in range(4):
        num = num + hw[4 + p, 4:8] * sf1[p]
    sg1[0:1] = jnp.sum(num, axis=0, keepdims=True)
    sg1[1:2] = jnp.sum(den, axis=0, keepdims=True)

    def broadcast(mine, got, count, offset_of, k):
        for n in sorted(range(1, count), key=lambda n: abs(n - count // 2)):
            copy = pltpu.make_async_remote_copy(src_ref=mine, dst_ref=got.at[n - 1], send_sem=gsem.at[2 * k], recv_sem=gsem.at[2 * k + 1],
                                                device_id=dev(*offset_of(n)), device_id_type=MESH)
            copy.start()
        return pltpu.make_async_remote_copy(src_ref=got, dst_ref=got, send_sem=gsem.at[2 * k], recv_sem=gsem.at[2 * k + 1],
                                            device_id=dev(*offset_of(1)), device_id_type=MESH)

    pl.semaphore_wait(far, 2)
    all_y = broadcast(sg1, rg1, NYD, lambda n: (0, n), 0)

    for w in wait_f1:
        w.wait_recv()
    spread1(sf1, rf1, f1)
    first(lev1, f1, v1a, 1, 11)
    second(lev1, f1, v1a, v1b, 2, 10)
    residual(lev1, f1, v1b, r1b, 4, 8)
    f2own = rdot(ldot(lr1, r1b[...].reshape(64, 128)), rz1[...])
    g0 = f2own[0:2] * lev2.iv[H2, H2 : H2 + 2] * mid2
    g1 = f2own[2:4] * lev2.iv[H2 + 1, H2 : H2 + 2] * mid2
    sf2[...] = g0 + pltpu.roll(g1, 64, 1)
    wait_f2 = [send(sf2, gf2.at[R2 - k], 0, k) for k in offs]
    for p in range(4):
        su1[p] = v1b[4 + p, 4:8]
    wait_u1 = [send(su1, ru1.at[n], a, b) for n, (a, b) in enumerate(NEAR)]

    ones = jnp.concatenate([mask2(i) for i in range(5, 13)], axis=0)
    y1[...] = rdot(ldot(lp1[...], ones), pz1[...]).reshape(12, 16, 128)
    post(lev1, None, y1, v1a, 1, 11)
    y0[2:14] = rdot(ldot(lp0[...], y1[2:10].reshape(128, 128)), pz0[...]).reshape(12, 16, 256)
    post(lev0, None, y0, v0a, 3, 13, yout)

    for w in wait_f2:
        w.wait_recv()
    gather2(sf2, gf2, af2)
    wait_f2 = [send(af2, rf2.at[R2 - k], k, 0) for k in offx]

    all_y.wait_recv()
    sg2[...] = sg1[...] + jnp.sum(rg1[...], axis=0)
    all_x = broadcast(sg2, rg2, NXD, lambda n: (n, 0), 1)

    for w in wait_u1:
        w.wait_recv()
    spread1(su1, ru1, u1)
    for i in range(12):
        u1[i] = u1[i] * mask1(i)

    for w in wait_u0:
        w.wait_recv()
    for p in range(8):
        v0b[4 + p, 2:4] = ruy[0, p]
        v0b[4 + p, 12:14] = ruy[1, p]
    for i in (2, 3, 12, 13):
        v0b[i] = zed
    for p in range(2):
        v0b[2 + p, 4:12] = rux[0, p]
        v0b[12 + p, 4:12] = rux[1, p]
    for s in (0, 1):
        v0b[3, 2 + 10 * s : 4 + 10 * s] = ruc[0, s]
        v0b[12, 2 + 10 * s : 4 + 10 * s] = ruc[1, s]
    for i in range(2, 14):
        v0b[i] = v0b[i] * mask0(i)

    for w in wait_f2:
        w.wait_recv()
    unpack2(af2, rf2, v2a)
    for i in range(1, 17):
        d = v2a[i]
        d2[i] = d
        f2[i] = d * (lev2.dg[i] * (1.0 / mid2))
    va, vb = v2a, v2b
    for m, (k2, p2) in enumerate(pairs2):
        for i in range(1 + m, 17 - m):
            r = f2[i] - lev2.apply(va, i)
            d = k2 * d2[i] + p2 * (r * lev2.iv[i])
            d2[i] = d
            vb[i] = va[i] + d
        va, vb = vb, va

    p1 = rdot(ldot(lp1[...], va[5:13].reshape(192, 128)), pz1[...]).reshape(12, 16, 128)
    for i in range(12):
        u1[i] = u1[i] + p1[i]
    post(lev1, f1, u1, v1a, 1, 11)
    p0 = rdot(ldot(lp0[...], u1[2:10].reshape(128, 128)), pz0[...]).reshape(12, 16, 256)
    for i in range(12):
        v0b[i + 2] = v0b[i + 2] + p0[i]
    post(lev0, f0, v0b, v0a, 3, 13, o_ref)

    all_x.wait_recv()
    total = sg2[...] + jnp.sum(rg2[...], axis=0)
    shift = jnp.sum(total[0:1], axis=1, keepdims=True) / jnp.sum(total[1:2], axis=1, keepdims=True)
    for p in range(8):
        o_ref[p] = o_ref[p] + shift * yout[p]
    all_y.wait_send()
    all_x.wait_send()

    for w in sends:
        w.wait_send()


def solution(mesh):
    def vm(*shape):
        return pltpu.VMEM(shape, F32)

    def level(*shape):
        return [vm(*shape) for _ in range(6)]

    nsend = 4 + 4 + 2 + 8 + 8 + 8 + 8 + 8 + 8 + 8 + 8
    scratch = [
        vm(8, 8, 256), vm(8, 8, 256), vm(2, 2, 8, 4, 256), vm(2, 2, 3, 2, 256), vm(2, 2, 8, 256), vm(2, 3, 8, 256), vm(2, 2, 8, 4, 256),
        vm(2, 2, 3, 2, 256), vm(2, 2, 8, 256), vm(2, 8, 2, 256), vm(2, 2, 8, 256), vm(2, 8, 2, 256), vm(2, 2, 2, 256),
        vm(16, 16, 256), vm(16, 16, 256), vm(16, 16, 256), level(16, 16, 256),
        vm(4, 4, 128), vm(8, 4, 4, 128), vm(4, 4, 128), vm(8, 4, 4, 128), vm(4, 4, 128), vm(8, 4, 4, 128),
        vm(12, 16, 128), vm(12, 16, 128), vm(12, 16, 128), vm(12, 16, 128), level(12, 16, 128),
        vm(2, 128), vm(9, 2, 128), vm(24, 128), vm(9, 24, 128), vm(2, 128), vm(9, 2, 128), vm(24, 128), vm(9, 24, 128),
        vm(18, 24, 128), vm(18, 24, 128), vm(18, 24, 128), vm(18, 24, 128), level(18, 24, 128),
        vm(8, 16, 256), vm(4, 16, 128), vm(192, 192), vm(192, 128), vm(256, 128), vm(128, 128), vm(128, 128), vm(128, 256),
        vm(12, 16, 128), vm(12, 16, 128), vm(12, 16, 128), vm(16, 16, 256), vm(8, 8, 256),
        vm(2, 128), vm(NYD - 1, 2, 128), vm(2, 128), vm(NXD - 1, 2, 128),
        pltpu.SemaphoreType.DMA((nsend,)), pltpu.SemaphoreType.DMA((nsend,)), pltpu.SemaphoreType.DMA((6,)), pltpu.SemaphoreType.REGULAR,
    ]

    def body(right_side, coefficient):
        return pl.pallas_call(
            body_kernel,
            out_shape=jax.ShapeDtypeStruct((8, 8, 256), F32),
            in_specs=[pl.BlockSpec(memory_space=pl.ANY)] * 2,
            out_specs=pl.BlockSpec(memory_space=pltpu.VMEM),
            scratch_shapes=scratch,
            compiler_params=pltpu.CompilerParams(collective_id=0, has_side_effects=True),
        )(right_side, coefficient)

    placed = (P("gx", "gy", None), P("gx", "gy", None))
    return jax.shard_map(body, mesh=mesh, in_specs=placed, out_specs=P("gx", "gy", None), check_vma=False)
```

```python
import jax
import jax.numpy as jnp
from jax import lax
from jax.experimental import pallas as pl
from jax.experimental.pallas import tpu as pltpu
from jax.sharding import PartitionSpec as P

SMOOTH_LOW = 0.5
SMOOTH_HIGH = 2.0
COARSE_LOW = 0.05
COARSE_HIGH = 2.0
COARSE_STEPS = 6

F32 = jnp.float32
NXD, NYD = 16, 32
NX, NY, NZ = 128, 256, 256
R2 = 4
H2 = 2 * R2
MESH = pl.DeviceIdType.MESH
NEAR = [(1, 1), (1, -1), (-1, 1), (-1, -1), (1, 0), (-1, 0), (0, 1), (0, -1)]


def chebyshev(low_end, high_end, sweeps):
    middle = 0.5 * (high_end + low_end)
    half_span = 0.5 * (high_end - low_end)
    sig_ratio = middle / half_span
    rho_now = 1.0 / sig_ratio
    pairs = []
    for _ in range(1, sweeps):
        rho_next = 1.0 / (2.0 * sig_ratio - rho_now)
        pairs.append((rho_next * rho_now, 2.0 * rho_next / half_span))
        rho_now = rho_next
    return 1.0 / middle, pairs


def iota(shape, dim):
    return lax.broadcasted_iota(jnp.int32, shape, dim)


def thirds(x):
    hi = x.astype(jnp.bfloat16)
    rest = x - hi.astype(F32)
    mid = rest.astype(jnp.bfloat16)
    return hi, mid, (rest - mid.astype(F32)).astype(jnp.bfloat16)


def ldot(w, x):
    w = w.astype(jnp.bfloat16)
    hi, mid, lo = (jnp.dot(w, t, preferred_element_type=F32) for t in thirds(x))
    return hi + (mid + lo)


def rdot(x, w):
    w = w.astype(jnp.bfloat16)
    hi, mid, lo = (jnp.dot(t, w, preferred_element_type=F32) for t in thirds(x))
    return hi + (mid + lo)


def up1(v):
    return pltpu.roll(v, v.shape[0] - 1, 0)


def dn1(v):
    return pltpu.roll(v, 1, 0)


def lup(v):
    return pltpu.roll(v, v.shape[1] - 1, 1)


def ldn(v):
    return pltpu.roll(v, 1, 1)


def interp(out_cell, in_cell):
    home = out_cell >> 1
    near = jnp.where((out_cell & 1) == 0, home - 1, home + 1)
    return jnp.where(in_cell == home, 0.75, 0.0).astype(F32) + jnp.where(in_cell == near, 0.25, 0.0).astype(F32)


def pair_sum(fine, coarse):
    r, c = iota((fine, coarse), 0), iota((fine, coarse), 1)
    return jnp.where((r >> 1) == c, 1.0, 0.0).astype(F32)


class Level:
    def __init__(self, refs, planes, rows, lanes, zfull):
        self.c, self.wx, self.wy, self.wz, self.dg, self.iv = refs
        self.planes, self.rows, self.lanes, self.zfull = planes, rows, lanes, zfull

    def build(self, mask_of, lo, hi):
        lane = iota((self.rows, self.lanes), 1)
        c = self.c[lo - 1]
        for i in range(lo - 1, hi):
            nxt = self.c[i + 1]
            wxp = 0.5 * (c + nxt)
            self.wx[i] = wxp
            if i >= lo:
                wyp = 0.5 * (c + up1(c))
                wym = dn1(wyp)
                if self.zfull:
                    wzp = 0.5 * (c + jnp.where(lane == self.lanes - 1, 0.0, lup(c)))
                    wzm = 0.5 * (c + jnp.where(lane == 0, 0.0, ldn(c)))
                    wz = jnp.where(lane == self.lanes - 1, 0.0, wzp)
                else:
                    wzp = 0.5 * (c + lup(c))
                    wzm = ldn(wzp)
                    wz = wzp
                diag = wxp + self.wx[i - 1] + wyp + wym + wzp + wzm
                m = mask_of(i)
                self.wy[i] = wyp
                self.wz[i] = wz
                self.dg[i] = diag
                self.iv[i] = m / jnp.where(diag > 0.0, diag, 1.0)
            c = nxt

    def apply(self, v, i):
        x = v[i]
        s = self.wx[i] * v[i + 1] + self.wx[i - 1] * v[i - 1]
        wy = self.wy[i]
        s = s + wy * up1(x) + dn1(wy * x)
        wz = self.wz[i]
        s = s + wz * lup(x) + ldn(wz * x)
        return self.dg[i] * x - s


def body_kernel(f_hbm, c_hbm, o_ref,
                f_ref, c_ref, sy, sc, rxf, rxc, ry, rc, sux, suy, rux, ruy, ruc, f0, v0a, v0b, l0,
                sc1, rc1, sf1, rf1, su1, ru1, f1, u1, v1a, v1b, l1,
                sc2, gc2, ac2, rc2, sf2, gf2, af2, rf2, f2, v2a, v2b, d2, l2,
                r0b, r1b, lp1, lp0, rz0, rz1, pz1, pz0, hw, hx, y1, y0, yout,
                sg1, rg1, sg2, rg2, ssem, rsem, gsem, far):
    mx, my = lax.axis_index("gx"), lax.axis_index("gy")

    def dev(a, b):
        return (lax.rem(mx + (a + NXD), NXD), lax.rem(my + (b + NYD), NYD))

    partners = [(a, b) for a, b in NEAR if a and b]
    partners += [(0, b) for b in range(-R2, R2 + 1) if b] + [(a, 0) for a in range(-R2, R2 + 1) if a]
    barrier = pltpu.get_barrier_semaphore()
    for a, b in partners:
        pl.semaphore_signal(barrier, inc=1, device_id=dev(a, b), device_id_type=MESH)

    get_c = pltpu.make_async_copy(c_hbm, c_ref, gsem.at[4])
    get_f = pltpu.make_async_copy(f_hbm, f_ref, gsem.at[5])
    get_c.start()
    get_f.start()
    sends = []

    def send(src, dst, a, b):
        k = len(sends)
        copy = pltpu.make_async_remote_copy(src_ref=src, dst_ref=dst, send_sem=ssem.at[k], recv_sem=rsem.at[k],
                                            device_id=dev(a, b), device_id_type=MESH)
        copy.start()
        sends.append(copy)
        return copy

    def pack2(v):
        return v[0:2] + pltpu.roll(v[2:4], 64, 1)

    o, q = iota((4, 64), 0), iota((4, 64), 1)
    lc2 = jnp.where(((q >> 5) == (o >> 1)) & (((q & 7) >> 2) == (o & 1)), 0.015625, 0.0).astype(F32)
    o, q = iota((256, 128), 0), iota((256, 128), 1)
    zc2 = jnp.where((o >> 2) == q, 1.0, 0.0).astype(F32)
    get_c.wait()
    sc2[...] = pack2(rdot(ldot(lc2, c_ref[...].reshape(64, 256)), zc2))
    get_f.wait()
    for p in range(8):
        fp, cp = f_ref[p], c_ref[p]
        for s in (0, 1):
            sy[s, 0, p] = fp[4 * s : 4 * s + 4]
            sy[s, 1, p] = cp[4 * s : 4 * s + 4]
    for sx in (0, 1):
        for s in (0, 1):
            sc[sx, s, 0] = c_ref[6 * sx, 6 * s : 6 * s + 2]
            sc[sx, s, 1] = c_ref[6 * sx + 1, 6 * s : 6 * s + 2]
            sc[sx, s, 2] = f_ref[7 * sx, 6 * s : 6 * s + 2]
    pl.semaphore_wait(barrier, len(partners))

    offs = [4, -4, 3, -3, 2, -2, 1, -1]
    offx = [2, -2, 3, -3, 1, -1, 4, -4]
    wait_c2 = [send(sc2, gc2.at[R2 - k], 0, k) for k in offs]
    wait_a = []
    for sx, a in ((1, 1), (0, -1)):
        for s, b in ((1, 1), (0, -1)):
            wait_a.append(send(sc.at[sx, s], rc.at[1 - sx, 1 - s], a, b))
    for s, a in ((1, 1), (0, -1)):
        wait_a.append(send(c_ref.at[5:8] if s else c_ref.at[0:3], rxc.at[1 - s], a, 0))
        wait_a.append(send(f_ref.at[6:8] if s else f_ref.at[0:2], rxf.at[1 - s], a, 0))
    for s, b in ((1, 1), (0, -1)):
        wait_a.append(send(sy.at[s], ry.at[1 - s], 0, b))
    rz0[...] = pair_sum(256, 128)
    rz1[...] = pair_sum(128, 128)
    o, q = iota((16, 64), 0), iota((16, 64), 1)
    lc1 = jnp.where(((q >> 4) == (o >> 2)) & (((q & 7) >> 1) == (o & 3)), 0.125, 0.0).astype(F32)
    sc1[...] = rdot(ldot(lc1, c_ref[...].reshape(64, 256)), rz0[...]).reshape(4, 4, 128)
    wait_c1 = [send(sc1, rc1.at[n], a, b) for n, (a, b) in enumerate(NEAR)]

    zed = jnp.zeros((16, 256), F32)
    for p in (0, 1, 2, 3, 12, 13, 14, 15):
        f0[p] = zed
        l0[0][p] = zed

    o, q = iota((16, 128), 0), iota((16, 128), 1)
    yr = (q & 15) - 4
    lr0 = jnp.where(((q >> 5) == (o >> 2)) & ((yr >> 1) == (o & 3)) & (yr >= 0) & (yr < 8), 0.5, 0.0).astype(F32)
    o, q = iota((4, 64), 0), iota((4, 64), 1)
    yr = (q & 15) - 4
    lr1 = jnp.where(((q >> 5) == (o >> 1)) & ((yr >> 1) == (o & 1)) & (yr >= 0) & (yr < 4), 0.5, 0.0).astype(F32)

    def prolong_matrix(planes_out, x_out0, x_in0, rows_in, planes_in, y_out0, y_in0, bx, by, nx, ny):
        shape = (planes_out * 16, planes_in * rows_in)
        r, c = iota(shape, 0), iota(shape, 1)
        xo, yo = (r >> 4) + x_out0, (r & 15) + y_out0
        if rows_in == 16:
            ci, cr = c >> 4, c & 15
        else:
            ci = (c * 2731) >> 16
            cr = c - ci * rows_in
        w = interp(xo, ci + x_in0) * interp(yo, cr + y_in0)
        gx_, gy_ = xo + mx * bx, yo + my * by
        ok = (gx_ >= 0) & (gx_ < nx) & (gy_ >= 0) & (gy_ < ny)
        return jnp.where(ok, w, 0.0)

    lp1[...] = prolong_matrix(12, -4, -3, 24, 8, -4, -H2, 4, 4, 64, 128)
    lp0[...] = prolong_matrix(12, -2, -2, 16, 8, -4, -4, 8, 8, 128, 256)
    r, c = iota((128, 128), 0), iota((128, 128), 1)
    pz1[...] = jnp.where(r < 64, interp(c, r), 0.0)
    r, c = iota((128, 256), 0), iota((128, 256), 1)
    pz0[...] = interp(c, r)

    def masker(rows, lanes, halo, b, nx, ny, valid_lanes, valid_rows):
        row = iota((rows, lanes), 0)
        y = row - halo + my * b
        ok = (y >= 0) & (y < ny) & (row < valid_rows)
        if valid_lanes < lanes:
            ok = ok & (iota((rows, lanes), 1) < valid_lanes)
        base = jnp.where(ok, 1.0, 0.0).astype(F32)

        def mask_of(i):
            x = mx * b + (i - halo)
            return base * jnp.where((x >= 0) & (x < nx), 1.0, 0.0).astype(F32)

        return mask_of

    mask0 = masker(16, 256, 4, 8, NX, NY, 256, 16)
    mask1 = masker(16, 128, 4, 4, NX // 2, NY // 2, 128, 12)
    mask2 = masker(24, 128, H2, 2, NX // 4, NY // 4, 64, 2 * H2 + 2)

    def gather2(mine, got, rows):
        rows[...] = jnp.zeros((24, 128), F32)
        rows[H2 : H2 + 2] = mine[...]
        for k in offs:
            rows[2 * (k + R2) : 2 * (k + R2) + 2] = got[k + R2]

    def unpack2(mine, got, cells):
        for k in [0] + offs:
            v = mine[...] if k == 0 else got[k + R2]
            i = 2 * (k + R2)
            cells[i] = v * mask2(i)
            cells[i + 1] = pltpu.roll(v, 64, 1) * mask2(i + 1)

    def spread1(mine, got, cells):
        for n, (a, b) in enumerate([(0, 0)] + NEAR):
            for p in range(4):
                x, y = 4 - 4 * a + p, 4 - 4 * b
                cells[x, y : y + 4] = mine[p] if n == 0 else got[n - 1, p]

    for w in wait_c2:
        w.wait_recv()
    for b in (8, -8):
        pl.semaphore_signal(far, inc=1, device_id=dev(0, b), device_id_type=MESH)
    gather2(sc2, gc2, ac2)
    wait_c2 = [send(ac2, rc2.at[R2 - k], k, 0) for k in offx]

    zed1 = jnp.zeros((4, 128), F32)
    for i in range(12):
        l1[0][i, 12:16] = zed1
        f1[i, 12:16] = zed1
        u1[i, 12:16] = zed1
    for w in wait_c1:
        w.wait_recv()
    spread1(sc1, rc1, l1[0])
    for i in range(12):
        l1[0][i] = l1[0][i] * mask1(i)
    lev1 = Level(l1, 12, 16, 128, True)
    lev1.build(mask1, 1, 11)

    for w in wait_a:
        w.wait_recv()
    c0 = l0[0]
    for p in range(8):
        i = p + 4
        f0[i, 0:4] = ry[0, 0, p]
        f0[i, 4:12] = f_ref[p]
        f0[i, 12:16] = ry[1, 0, p]
        c0[i, 0:4] = ry[0, 1, p]
        c0[i, 4:12] = c_ref[p]
        c0[i, 12:16] = ry[1, 1, p]
    for p in range(3):
        c0[1 + p, 4:12] = rxc[0, p]
        c0[12 + p, 4:12] = rxc[1, p]
    for p in range(2):
        f0[2 + p, 4:12] = rxf[0, p]
        f0[12 + p, 4:12] = rxf[1, p]
        for s in (0, 1):
            c0[2 + p, 2 + 10 * s : 4 + 10 * s] = rc[0, s, p]
            c0[12 + p, 2 + 10 * s : 4 + 10 * s] = rc[1, s, p]
    for s in (0, 1):
        f0[3, 2 + 10 * s : 4 + 10 * s] = rc[0, s, 2]
        f0[12, 2 + 10 * s : 4 + 10 * s] = rc[1, s, 2]
    for i in range(16):
        c0[i] = c0[i] * mask0(i)
    lev0 = Level(l0, 16, 16, 256, True)
    lev0.build(mask0, 2, 14)

    inv_mid, ((keep, push),) = chebyshev(SMOOTH_LOW, SMOOTH_HIGH, 2)

    def first(lev, f, v, lo, hi):
        for i in range(lo, hi):
            v[i] = f[i] * lev.iv[i] * inv_mid

    def second(lev, f, va, vb, lo, hi):
        for i in range(lo, hi):
            d = va[i]
            r = f[i] - lev.apply(va, i)
            vb[i] = d + (keep * d + push * (r * lev.iv[i]))

    def residual(lev, f, v, out, lo, hi):
        for i in range(lo, hi):
            out[i - lo] = f[i] - lev.apply(v, i)

    first(lev0, f0, v0a, 2, 14)
    second(lev0, f0, v0a, v0b, 3, 13)
    residual(lev0, f0, v0b, r0b, 4, 12)
    f1own = rdot(ldot(lr0, r0b[...].reshape(128, 256)), rz0[...])
    sf1[...] = f1own.reshape(4, 4, 128)
    wait_f1 = [send(sf1, rf1.at[n], a, b) for n, (a, b) in enumerate(NEAR)]

    for p in range(8):
        for s in (0, 1):
            suy[s, p] = v0b[4 + p, 4 + 6 * s : 6 + 6 * s]
    for p in range(2):
        for s in (0, 1):
            sux[s, p] = v0b[4 + 6 * s + p, 4:12]
    wait_u0 = []
    for sx, a in ((1, 1), (0, -1)):
        for s, b in ((1, 1), (0, -1)):
            wait_u0.append(send(suy.at[s, 7 * sx], ruc.at[1 - sx, 1 - s], a, b))
    wait_u0 += [send(sux.at[s], rux.at[1 - s], a, 0) for s, a in ((1, 1), (0, -1))]
    wait_u0 += [send(suy.at[s], ruy.at[1 - s], 0, b) for s, b in ((1, 1), (0, -1))]

    for w in wait_c2:
        w.wait_recv()
    unpack2(ac2, rc2, l2[0])
    lev2 = Level(l2, 18, 24, 128, False)
    lev2.build(mask2, 1, 17)

    def rhs(lev, f, v, i):
        return -lev.apply(v, i) if f is None else f[i] - lev.apply(v, i)

    def post(lev, f, v, w, lo, hi, out=None):
        for i in range(lo, hi):
            w[i] = v[i] + rhs(lev, f, v, i) * lev.iv[i] * inv_mid
        for i in range(lo + 1, hi - 1):
            d = w[i] - v[i]
            e = w[i] + (keep * d + push * (rhs(lev, f, w, i) * lev.iv[i]))
            if out is None:
                v[i] = e
            else:
                out[i - lo - 1] = e[4:12]

    mid2, pairs2 = chebyshev(COARSE_LOW, COARSE_HIGH, COARSE_STEPS)
    row = iota((24, 128), 0)
    own = jnp.where((row == H2) | (row == H2 + 1), 1.0, 0.0).astype(F32)
    for i in range(1, 17):
        v2a[i] = mask2(i)
    den = jnp.zeros((24, 128), F32)
    va, vb = v2a, v2b
    for m, (k2, p2) in enumerate([(0.0, mid2)] + pairs2):
        for i in range(2 + m, 16 - m):
            r = lev2.apply(va, i)
            if m == 0 and i in (H2, H2 + 1):
                den = den + own * mask2(i) * r
            d = -p2 * (r * lev2.iv[i])
            if m:
                d = k2 * d2[i] + d
            d2[i] = d
            vb[i] = va[i] + d
        va, vb = vb, va
    r, c = iota((128, 96), 0), iota((128, 96), 1)
    ci = (c * 2731) >> 16
    spread = ((((r >> 4) - 2) >> 1) == ci - 1) & ((((r & 15) - 4) >> 1) == c - ci * 24 - H2)
    spread = jnp.where(spread, 0.5, 0.0).astype(F32)
    r, c = iota((128, 128), 0), iota((128, 128), 1)
    hw[2:10] = rdot(ldot(spread, va[7:11].reshape(96, 128)), jnp.where((c >> 1) == r, 1.0, 0.0).astype(F32)).reshape(8, 16, 128)
    post(lev1, None, hw, hx, 3, 9)
    num = jnp.zeros((4, 128), F32)
    for p in range(4):
        num = num + hw[4 + p, 4:8] * sf1[p]
    sg1[0:1] = jnp.sum(num, axis=0, keepdims=True)
    sg1[1:2] = jnp.sum(den, axis=0, keepdims=True)

    def broadcast(mine, got, count, offset_of, k):
        for n in sorted(range(1, count), key=lambda n: abs(n - count // 2)):
            copy = pltpu.make_async_remote_copy(src_ref=mine, dst_ref=got.at[n - 1], send_sem=gsem.at[2 * k], recv_sem=gsem.at[2 * k + 1],
                                                device_id=dev(*offset_of(n)), device_id_type=MESH)
            copy.start()
        return pltpu.make_async_remote_copy(src_ref=got, dst_ref=got, send_sem=gsem.at[2 * k], recv_sem=gsem.at[2 * k + 1],
                                            device_id=dev(*offset_of(1)), device_id_type=MESH)

    pl.semaphore_wait(far, 2)
    all_y = broadcast(sg1, rg1, NYD, lambda n: (0, n), 0)

    for w in wait_f1:
        w.wait_recv()
    spread1(sf1, rf1, f1)
    first(lev1, f1, v1a, 1, 11)
    second(lev1, f1, v1a, v1b, 2, 10)
    residual(lev1, f1, v1b, r1b, 4, 8)
    f2own = rdot(ldot(lr1, r1b[...].reshape(64, 128)), rz1[...])
    g0 = f2own[0:2] * lev2.iv[H2, H2 : H2 + 2] * mid2
    g1 = f2own[2:4] * lev2.iv[H2 + 1, H2 : H2 + 2] * mid2
    sf2[...] = g0 + pltpu.roll(g1, 64, 1)
    wait_f2 = [send(sf2, gf2.at[R2 - k], 0, k) for k in offs]
    for p in range(4):
        su1[p] = v1b[4 + p, 4:8]
    wait_u1 = [send(su1, ru1.at[n], a, b) for n, (a, b) in enumerate(NEAR)]

    ones = jnp.concatenate([mask2(i) for i in range(5, 13)], axis=0)
    y1[...] = rdot(ldot(lp1[...], ones), pz1[...]).reshape(12, 16, 128)
    post(lev1, None, y1, v1a, 1, 11)
    y0[2:14] = rdot(ldot(lp0[...], y1[2:10].reshape(128, 128)), pz0[...]).reshape(12, 16, 256)
    post(lev0, None, y0, v0a, 3, 13, yout)

    for w in wait_f2:
        w.wait_recv()
    gather2(sf2, gf2, af2)
    wait_f2 = [send(af2, rf2.at[R2 - k], k, 0) for k in offx]

    all_y.wait_recv()
    sg2[...] = sg1[...] + jnp.sum(rg1[...], axis=0)
    all_x = broadcast(sg2, rg2, NXD, lambda n: (n, 0), 1)

    for w in wait_u1:
        w.wait_recv()
    spread1(su1, ru1, u1)
    for i in range(12):
        u1[i] = u1[i] * mask1(i)

    for w in wait_u0:
        w.wait_recv()
    for p in range(8):
        v0b[4 + p, 2:4] = ruy[0, p]
        v0b[4 + p, 12:14] = ruy[1, p]
    for i in (2, 3, 12, 13):
        v0b[i] = zed
    for p in range(2):
        v0b[2 + p, 4:12] = rux[0, p]
        v0b[12 + p, 4:12] = rux[1, p]
    for s in (0, 1):
        v0b[3, 2 + 10 * s : 4 + 10 * s] = ruc[0, s]
        v0b[12, 2 + 10 * s : 4 + 10 * s] = ruc[1, s]
    for i in range(2, 14):
        v0b[i] = v0b[i] * mask0(i)

    for w in wait_f2:
        w.wait_recv()
    unpack2(af2, rf2, v2a)
    for i in range(1, 17):
        d = v2a[i]
        d2[i] = d
        f2[i] = d * (lev2.dg[i] * (1.0 / mid2))
    va, vb = v2a, v2b
    for m, (k2, p2) in enumerate(pairs2):
        for i in range(1 + m, 17 - m):
            r = f2[i] - lev2.apply(va, i)
            d = k2 * d2[i] + p2 * (r * lev2.iv[i])
            d2[i] = d
            vb[i] = va[i] + d
        va, vb = vb, va

    p1 = rdot(ldot(lp1[...], va[5:13].reshape(192, 128)), pz1[...]).reshape(12, 16, 128)
    for i in range(12):
        u1[i] = u1[i] + p1[i]
    post(lev1, f1, u1, v1a, 1, 11)
    p0 = rdot(ldot(lp0[...], u1[2:10].reshape(128, 128)), pz0[...]).reshape(12, 16, 256)
    for i in range(12):
        v0b[i + 2] = v0b[i + 2] + p0[i]
    post(lev0, f0, v0b, v0a, 3, 13, o_ref)

    all_x.wait_recv()
    total = sg2[...] + jnp.sum(rg2[...], axis=0)
    shift = jnp.sum(total[0:1], axis=1, keepdims=True) / jnp.sum(total[1:2], axis=1, keepdims=True)
    for p in range(8):
        o_ref[p] = o_ref[p] + shift * yout[p]
    all_y.wait_send()
    all_x.wait_send()

    for w in sends:
        w.wait_send()


def solution(mesh):
    def vm(*shape):
        return pltpu.VMEM(shape, F32)

    def level(*shape):
        return [vm(*shape) for _ in range(6)]

    nsend = 4 + 4 + 2 + 8 + 8 + 8 + 8 + 8 + 8 + 8 + 8
    scratch = [
        vm(8, 8, 256), vm(8, 8, 256), vm(2, 2, 8, 4, 256), vm(2, 2, 3, 2, 256), vm(2, 2, 8, 256), vm(2, 3, 8, 256), vm(2, 2, 8, 4, 256),
        vm(2, 2, 3, 2, 256), vm(2, 2, 8, 256), vm(2, 8, 2, 256), vm(2, 2, 8, 256), vm(2, 8, 2, 256), vm(2, 2, 2, 256),
        vm(16, 16, 256), vm(16, 16, 256), vm(16, 16, 256), level(16, 16, 256),
        vm(4, 4, 128), vm(8, 4, 4, 128), vm(4, 4, 128), vm(8, 4, 4, 128), vm(4, 4, 128), vm(8, 4, 4, 128),
        vm(12, 16, 128), vm(12, 16, 128), vm(12, 16, 128), vm(12, 16, 128), level(12, 16, 128),
        vm(2, 128), vm(9, 2, 128), vm(24, 128), vm(9, 24, 128), vm(2, 128), vm(9, 2, 128), vm(24, 128), vm(9, 24, 128),
        vm(18, 24, 128), vm(18, 24, 128), vm(18, 24, 128), vm(18, 24, 128), level(18, 24, 128),
        vm(8, 16, 256), vm(4, 16, 128), vm(192, 192), vm(192, 128), vm(256, 128), vm(128, 128), vm(128, 128), vm(128, 256),
        vm(12, 16, 128), vm(12, 16, 128), vm(12, 16, 128), vm(16, 16, 256), vm(8, 8, 256),
        vm(2, 128), vm(NYD - 1, 2, 128), vm(2, 128), vm(NXD - 1, 2, 128),
        pltpu.SemaphoreType.DMA((nsend,)), pltpu.SemaphoreType.DMA((nsend,)), pltpu.SemaphoreType.DMA((6,)), pltpu.SemaphoreType.REGULAR,
    ]

    def body(right_side, coefficient):
        return pl.pallas_call(
            body_kernel,
            out_shape=jax.ShapeDtypeStruct((8, 8, 256), F32),
            in_specs=[pl.BlockSpec(memory_space=pl.ANY)] * 2,
            out_specs=pl.BlockSpec(memory_space=pltpu.VMEM),
            scratch_shapes=scratch,
            compiler_params=pltpu.CompilerParams(collective_id=0, has_side_effects=True),
        )(right_side, coefficient)

    placed = (P("gx", "gy", None), P("gx", "gy", None))
    return jax.shard_map(body, mesh=mesh, in_specs=placed, out_specs=P("gx", "gy", None), check_vma=False)
```
